128 devices in a mesh: depth: 8 (over x, z_lo), width: 2 (over z_hi), hidden: 8 (over y, core).
Axes of the slice: x: 4, y: 4, z: 4 (z_hi: 2, z_lo: 2; z = z_hi * 2 + z_lo), core: 2. Of those that a mesh axis runs over, the one named last changes fastest.
Arguments:
- inputs: float32 [8192, 3072], P('depth', 'width'), may hold values from -6 to 6
- weight: float32 [3072, 12288], P('width', ('hidden', 'depth')), may hold values from -0.3125 to 0.3125
- cotangent: float32 [8192, 12288], P('depth', 'hidden'), may hold values from -6 to 6
Outputs:
- input_grad: float32 [8192, 3072], P('depth', ('width', 'hidden'))
- weight_grad: float32 [3072, 12288], P('width', ('hidden', 'depth'))
The draws below stay inside these ranges and needn't reach their ends.
All inputs are finite; a program needn't handle non-finite values.
Results may differ from the reference program's by a relative error of at most 0.00011.
Values sent between devices are 32-bit elements; how exact they have to be, the bound alone decides.
A program may use at most 192 MiB of HBM per device.

```python
import jax
import jax.numpy as jnp
from jax import lax

D = 3072
F = 12288
TOKENS = 8192


def strengthened(entries, key, source, target, parts, factor):
    def block_of(position):
        return (jnp.arange(entries.shape[position]) // (entries.shape[position] // parts)).reshape((-1,) + (1,) * (entries.ndim - 1 - position))

    near = jax.random.permutation(key, parts)[block_of(target)]
    other_side = (block_of(target) + parts // 2) % parts
    return jnp.where((block_of(source) == near) | (block_of(source) == other_side), factor * entries, entries)


def level_of(rng, extent, shards, smallest, largest):
    def one(dim, shards_of):
        steps = jax.random.uniform(jax.random.fold_in(jax.random.fold_in(rng, 6), dim), (shards_of,), jnp.float32, smallest / len(shards), largest / len(shards))
        return jnp.repeat(jnp.exp(steps), extent[dim] // shards_of).reshape((-1,) + (1,) * (len(extent) - dim - 1))

    factor_of = one(*shards[0])
    for cut in shards[1:]:
        factor_of = factor_of * one(*cut)
    return factor_of


def scatter_about(stream_key, extent, scale, reach, split=(), kind=jnp.bfloat16):
    loudness = level_of(stream_key, extent, split, -0.22, 0.18) if split else 1.0
    entries = jax.random.normal(stream_key, extent, jnp.float32) * scale * loudness
    return jnp.minimum(jnp.maximum(entries, -reach), reach).astype(kind)


def noise_with(key, extent, deviation, bound, split, heavy, dtype=jnp.bfloat16):
    result = deviation * jax.random.normal(key, extent, jnp.float32)
    if split:
        result = result * level_of(key, extent, split, -0.22, 0.18)
    return jnp.clip(strengthened(result, jax.random.fold_in(key, 3), *heavy), -bound, bound).astype(dtype)


def setup_inputs(seed: int = 0) -> dict:
    streams_of = jax.random.split(jax.random.key(seed), 4)
    return {
        "inputs": scatter_about(streams_of[0], (TOKENS, D), 1.0, 6.0, ((0, 8), (1, 2)), jnp.float32),
        "weight": noise_with(streams_of[1], (D, F), D ** -0.5, 0.3125, ((0, 2), (1, 64)), (1, 0, 64, 4.0), jnp.float32),
        "cotangent": noise_with(streams_of[2], (TOKENS, F), 1.0, 6.0, ((0, 8), (1, 8)), (0, 1, 8, 2.0), jnp.float32),
    }


inv_sqrt_two = 0.7071067811865476
inv_sqrt_two_pi = 0.3989422804014327

def gelu_slope(preact):
    cumulative = 0.5 * (1.0 + jax.scipy.special.erf(preact * inv_sqrt_two))
    density = jnp.exp(-0.5 * preact * preact) * inv_sqrt_two_pi
    return cumulative + preact * density

def reference(inputs, weight, cotangent):
    preact = jnp.dot(inputs, weight, precision=lax.Precision.HIGHEST, preferred_element_type=jnp.float32)
    pre_grad = cotangent * gelu_slope(preact)
    input_grad = jnp.dot(pre_grad, weight.T, precision=lax.Precision.HIGHEST, preferred_element_type=jnp.float32)
    weight_grad = jnp.dot(inputs.T, pre_grad, precision=lax.Precision.HIGHEST, preferred_element_type=jnp.float32)
    return (input_grad, weight_grad)
```

```python
import jax
import jax.numpy as jnp
from jax import lax
from jax.experimental import pallas as pl
from jax.experimental.pallas import tpu as pltpu
from jax.sharding import Mesh
from jax.sharding import PartitionSpec as P

AXES = ("x", "zl", "zh", "y", "c")
MESH = pl.DeviceIdType.MESH
PIECES = 3

inv_sqrt_two = 0.7071067811865476
inv_sqrt_two_pi = 0.3989422804014327


class Place:
    def __init__(self):
        self.x, self.zl, self.zh, self.y, self.c = (lax.axis_index(a) for a in AXES)
        self.z = 2 * self.zh + self.zl
        self.inner = self.zl != self.zh
        self.outer = self.zl == self.zh
        self.to_inner = self.z + 1 - 2 * self.zh
        self.to_outer = 3 * self.zh

    def at_z(self, z):
        return (self.x, lax.rem(z, 2), lax.div(z, 2), self.y, self.c)

    def step(self, dx=0, dy=0, dz=0, dc=0):
        z = lax.rem(self.z + dz + 4, 4)
        return (
            lax.rem(self.x + dx + 4, 4),
            lax.rem(z, 2),
            lax.div(z, 2),
            lax.rem(self.y + dy + 4, 4),
            lax.rem(self.c + dc, 2),
        )


def enter(me):
    barrier = pltpu.get_barrier_semaphore()
    steps = [
        dict(dx=1), dict(dx=-1), dict(dy=1), dict(dy=-1),
        dict(dz=1), dict(dz=-1), dict(dz=2), dict(dc=1),
    ]
    for step in steps:
        pl.semaphore_signal(barrier, inc=1, device_id=me.step(**step), device_id_type=MESH)
    pl.semaphore_wait(barrier, len(steps))


def remote(src, dst, send, recv, device):
    return pltpu.make_async_remote_copy(
        src_ref=src, dst_ref=dst, send_sem=send, recv_sem=recv, device_id=device, device_id_type=MESH
    )


def gather_kernel(xh, wt, xo, wf, zs, zr, fs, xs, xr, gs, gr, s1, r1, sy, ry, sf, rf, sc, rc):
    me = Place()
    rows = wt.shape[0] // PIECES
    tok = xh.shape[0] // 8
    half = tok // 2

    def piece(p):
        return pl.ds(p * rows, rows)

    enter(me)
    slot = me.inner.astype(jnp.int32)
    for p in range(PIECES):
        remote(wt.at[piece(p)], wf.at[me.x, slot, piece(p)], zs.at[p], zr.at[slot, p], me.at_z(me.to_inner)).start()

        @pl.when(me.outer)
        def _():
            pltpu.make_async_copy(wt.at[piece(p)], wf.at[me.x, 0, piece(p)], zr.at[0, p]).start()

    def part(y, c):
        return pl.ds((y * 2 + c) * tok, tok)

    mine = part(me.y, me.c)
    first = remote(xh.at[mine], xo.at[mine], s1, r1, me.step(dz=2))
    first.start()

    for k in range(2 * PIECES):
        s = jnp.where(me.inner, k % 2, k // PIECES)
        p = jnp.where(me.inner, k // 2, k % PIECES)
        here = wf.at[me.x, s, piece(p)]
        pltpu.make_async_copy(here, here, zr.at[s, p]).wait()

        @pl.when(me.inner & (s == 1))
        def _():
            remote(here, here, fs.at[p], zr.at[s, p], me.at_z(me.to_outer)).start()

        for d, dx in enumerate((1, -1)):
            remote(here, here, xs.at[d, s, p], xr.at[d, s, p], me.step(dx=dx)).start()

    first.wait()
    across = [remote(xo.at[mine], xo.at[mine], sy.at[d], ry.at[d], me.step(dy=dy)) for d, dy in enumerate((1, -1))]
    for copy in across:
        copy.start()
    shares = [remote(xo.at[mine], xo.at[mine], sc.at[0], rc.at[0], me.step(dc=1))]
    shares[0].start()

    def pass_on(p):
        for d, dx in enumerate((1, -1)):
            there = wf.at[lax.rem(me.x - dx + 4, 4), d, piece(p)]
            remote(there, there, gs.at[d, p], xr.at[d, d, p], me.step(dx=dx)).wait_recv()
            remote(there, there, gs.at[d, p], gr.at[d, p], me.step(dx=dx)).start()

    pass_on(0)
    halves = []
    for d, dy in enumerate((1, -1)):
        across[d].wait_recv()
        from_y = lax.rem(me.y - dy + 4, 4)
        rows_of = pl.ds((from_y * 2 + me.c) * tok + d * half, half)
        halves.append(remote(xo.at[rows_of], xo.at[rows_of], sf.at[d], rf.at[d], me.step(dy=dy)))
        halves[-1].start()
        whole = part(from_y, me.c)
        shares.append(remote(xo.at[whole], xo.at[whole], sc.at[1 + d], rc.at[1 + d], me.step(dc=1)))
        shares[-1].start()
    for p in range(1, PIECES):
        pass_on(p)
    far = part(lax.rem(me.y + 2, 4), me.c)
    for d in range(2):
        halves[d].wait_recv()
    shares.append(remote(xo.at[far], xo.at[far], sc.at[3], rc.at[3], me.step(dc=1)))
    shares[-1].start()

    for p in range(PIECES):
        remote(wt.at[piece(p)], wt.at[piece(p)], zs.at[p], zs.at[p], me.step(dc=1)).wait_send()

        @pl.when(me.inner)
        def _():
            remote(wt.at[piece(p)], wt.at[piece(p)], fs.at[p], fs.at[p], me.step(dc=1)).wait_send()

        for d in range(2):
            for s in range(2):
                copy = remote(wt.at[piece(p)], wt.at[piece(p)], xs.at[d, s, p], xr.at[d, s, p], me.step(dc=1))
                copy.wait_send()
                if s != d:
                    copy.wait_recv()
            remote(wt.at[piece(p)], wt.at[piece(p)], gs.at[d, p], gr.at[d, p], me.step(dc=1)).wait()
    for d in range(2):
        across[d].wait_send()
        halves[d].wait_send()
    for copy in shares:
        copy.wait()


def gather(inputs, wt):
    dma = pltpu.SemaphoreType.DMA
    any_space = pl.BlockSpec(memory_space=pltpu.HBM)
    return pl.pallas_call(
        gather_kernel,
        out_shape=(
            jax.ShapeDtypeStruct(inputs.shape, jnp.float32),
            jax.ShapeDtypeStruct((4, 2) + wt.shape, jnp.float32),
        ),
        in_specs=[any_space, any_space],
        out_specs=(any_space, any_space),
        scratch_shapes=[
            dma((PIECES,)), dma((2, PIECES)), dma((PIECES,)),
            dma((2, 2, PIECES)), dma((2, 2, PIECES)),
            dma((2, PIECES)), dma((2, PIECES)),
            dma, dma, dma((2,)), dma((2,)), dma((2,)), dma((2,)), dma((4,)), dma((4,)),
        ],
        compiler_params=pltpu.CompilerParams(collective_id=0, has_side_effects=True),
    )(inputs, wt)


def reduce_kernel(
    dw, dx, wout, xout, far, near, v, zin, zsum, cin, acc, yfar, ynear, xz,
    fs, fr, ns, nr, zs, zr, os_, cs, cr, yfs, yfr, yns, ynr, s1, r1,
):
    me = Place()
    rows = wout.shape[0] // PIECES

    def piece(p):
        return pl.ds(p * rows, rows)

    def x_at(d):
        return lax.rem(me.x + d + 4, 4)

    def y_at(d):
        return lax.rem(me.y + d + 4, 4)

    enter(me)
    dirs = ((0, 1), (1, -1))
    opposite = []
    straight = []
    for p in range(PIECES):
        for d, step in dirs:
            copy = remote(dw.at[x_at(2), d, piece(p)], far.at[d, piece(p)], fs.at[d, p], fr.at[d, p], me.step(dx=step))
            copy.start()
            opposite.append(copy)
    shares = []
    for i, (s, dy) in enumerate(((0, 2), (1, 2), (0, 1), (1, -1), (1, 1), (0, -1), (0, 0), (1, 0))):
        copy = remote(dx.at[s, y_at(dy), 1 - me.c], cin.at[s, y_at(dy)], cs.at[i], cr.at[i], me.step(dc=1))
        copy.start()
        shares.append((copy, s, dy))
    for p in range(PIECES):
        for d, step in dirs:
            copy = remote(
                dw.at[x_at(step), 1 - d, piece(p)], near.at[d, 1 - d, piece(p)],
                ns.at[d, 1 - d, p], nr.at[d, 1 - d, p], me.step(dx=step),
            )
            copy.start()
            straight.append(copy)

    def on_chip(i):
        copy, s, dy = shares[i]
        copy.wait_recv()
        acc[s, y_at(dy)] = dx[s, y_at(dy), me.c] + cin[s, y_at(dy)]

    y_copies = []
    for d, step in dirs:
        on_chip(d)
        copy = remote(acc.at[d, y_at(2)], yfar.at[d], yfs.at[d], yfr.at[d], me.step(dy=step))
        copy.start()
        y_copies.append(copy)
    for i in range(2, 6):
        on_chip(i)
    for d, step in dirs:
        copy = remote(
            acc.at[1 - d, y_at(step)], ynear.at[d, 1 - d], yns.at[d, 1 - d], ynr.at[d, 1 - d], me.step(dy=step)
        )
        copy.start()
        y_copies.append(copy)
    for i in range(6, 8):
        on_chip(i)

    def pass_on(p):
        for d, step in dirs:
            opposite[2 * p + d].wait_recv()
            far[d, piece(p)] = far[d, piece(p)] + dw[x_at(step), d, piece(p)]
            copy = remote(
                far.at[d, piece(p)], near.at[d, d, piece(p)], ns.at[d, d, p], nr.at[d, d, p], me.step(dx=step)
            )
            copy.start()
            straight.append(copy)

    pass_on(0)
    pass_on(1)
    for d, step in dirs:
        y_copies[d].wait_recv()
        yfar[d] = yfar[d] + acc[d, y_at(step)]
        copy = remote(yfar.at[d], ynear.at[d, d], yns.at[d, d], ynr.at[d, d], me.step(dy=step))
        copy.start()
        y_copies.append(copy)
    pass_on(2)

    for d in range(2):
        y_copies[2 + d].wait_recv()
        y_copies[4 + d].wait_recv()
    acc[1, me.y] = acc[1, me.y] + ynear[0, 1] + ynear[1, 1]
    last = remote(acc.at[1, me.y], xz, s1, r1, me.step(dz=2))
    last.start()

    z_copies = []
    outs = []
    for p in range(PIECES):
        for d in range(2):
            straight[2 * p + d].wait_recv()
            straight[2 * PIECES + 2 * p + d].wait_recv()
        for s in range(2):
            v[s, piece(p)] = dw[me.x, s, piece(p)] + near[0, s, piece(p)] + near[1, s, piece(p)]

        @pl.when(me.outer)
        def _():
            remote(v.at[1, piece(p)], zin.at[0, piece(p)], zs.at[p], zr.at[0, p], me.at_z(me.to_inner)).start()

        @pl.when(me.inner)
        def _():
            remote(v.at[0, piece(p)], zin.at[1, piece(p)], zs.at[p], zr.at[1, p], me.at_z(me.to_outer)).start()

    for p in range(PIECES):
        @pl.when(me.inner)
        def _():
            remote(v.at[1, piece(p)], zin.at[0, piece(p)], os_.at[p], zr.at[0, p], me.at_z(me.to_inner)).wait_recv()
            zsum[piece(p)] = v[1, piece(p)] + zin[0, piece(p)]
            remote(zsum.at[piece(p)], zin.at[1, piece(p)], os_.at[p], zr.at[1, p], me.at_z(me.to_inner)).start()

    xout[...] = acc[0, me.y] + ynear[0, 0] + ynear[1, 0]
    last.wait_recv()
    xout[...] = xout[...] + xz[...]
    for p in range(PIECES):
        remote(v.at[1, piece(p)], zin.at[1, piece(p)], zs.at[p], zr.at[1, p], me.step(dz=1)).wait_recv()
        wout[piece(p)] = jnp.where(me.outer, v[0, piece(p)] + zin[1, piece(p)], zin[1, piece(p)])

    for p in range(PIECES):
        remote(v.at[1, piece(p)], zin.at[1, piece(p)], zs.at[p], zr.at[1, p], me.step(dz=1)).wait_send()

        @pl.when(me.inner)
        def _():
            remote(v.at[1, piece(p)], zin.at[0, piece(p)], os_.at[p], zr.at[0, p], me.step(dz=1)).wait_send()

    for copy in opposite + straight + y_copies + [s[0] for s in shares] + [last]:
        copy.wait_send()


def reduce(dw, dx):
    dma = pltpu.SemaphoreType.DMA
    vmem = pltpu.VMEM
    f32 = jnp.float32
    _, _, r, d = dw.shape
    _, _, _, b, t = dx.shape
    spec = pl.BlockSpec(memory_space=pltpu.VMEM)
    return pl.pallas_call(
        reduce_kernel,
        out_shape=(jax.ShapeDtypeStruct((r, d), f32), jax.ShapeDtypeStruct((b, t), f32)),
        in_specs=[spec, spec],
        out_specs=(spec, spec),
        scratch_shapes=[
            vmem((2, r, d), f32), vmem((2, 2, r, d), f32), vmem((2, r, d), f32), vmem((2, r, d), f32), vmem((r, d), f32),
            vmem((2, 4, b, t), f32), vmem((2, 4, b, t), f32), vmem((2, b, t), f32), vmem((2, 2, b, t), f32), vmem((b, t), f32),
            dma((2, PIECES)), dma((2, PIECES)), dma((2, 2, PIECES)), dma((2, 2, PIECES)),
            dma((PIECES,)), dma((2, PIECES)), dma((PIECES,)),
            dma((8,)), dma((8,)), dma((2,)), dma((2,)), dma((2, 2)), dma((2, 2)), dma, dma,
        ],
        compiler_params=pltpu.CompilerParams(collective_id=1, has_side_effects=True, vmem_limit_bytes=60 << 20),
    )(dw, dx)


def gelu_slope(preact):
    cumulative = 0.5 * (1.0 + jax.scipy.special.erf(preact * inv_sqrt_two))
    density = jnp.exp(-0.5 * preact * preact) * inv_sqrt_two_pi
    return cumulative + preact * density


def product(left, right, left_dim, right_dim):
    return lax.dot_general(
        left, right, (((left_dim,), (right_dim,)), ((), ())),
        precision=lax.Precision.HIGH, preferred_element_type=jnp.float32,
    )


def local(inputs, weight, cotangent):
    wt = weight.T
    r, d = wt.shape
    tok = inputs.shape[0]
    other, wf = gather(inputs, wt)
    near = wf[:, 0].reshape(4 * r, d)
    far = wf[:, 1].reshape(4 * r, d)
    cot = cotangent.reshape(tok, 4, 2, r)
    own = lax.dynamic_index_in_dim(cot, lax.axis_index("zh"), 2, keepdims=False).reshape(tok, 4 * r)
    preact = product(inputs, near, 1, 1) + product(other, far, 1, 1)
    pre_grad = own * gelu_slope(preact)
    dw = jnp.stack([product(pre_grad, half, 0, 0).reshape(4, r, d) for half in (inputs, other)], axis=1)
    dx = jnp.stack([product(half, pre_grad, 0, 1).reshape(4, 2, d // 8, tok) for half in (near, far)], axis=0)
    wout, xout = reduce(dw, dx)
    return (xout.T, wout.T)


def solution(mesh):
    torus = Mesh(mesh.devices.reshape(4, 2, 2, 4, 2), AXES)
    in_specs = (P(("x", "zl"), "zh"), P("zh", ("y", "c", "x", "zl")), P(("x", "zl"), ("y", "c")))
    out_specs = (P(("x", "zl"), ("zh", "y", "c")), P("zh", ("y", "c", "x", "zl")))
    return jax.shard_map(local, mesh=torus, in_specs=in_specs, out_specs=out_specs, check_vma=False)
```

```python
import jax
import jax.numpy as jnp
from jax import lax
from jax.experimental import pallas as pl
from jax.experimental.pallas import tpu as pltpu
from jax.sharding import Mesh
from jax.sharding import PartitionSpec as P

AXES = ("x", "zl", "zh", "y", "c")
MESH = pl.DeviceIdType.MESH
PIECES = 3

inv_sqrt_two = 0.7071067811865476
inv_sqrt_two_pi = 0.3989422804014327


class Place:
    def __init__(self):
        self.x, self.zl, self.zh, self.y, self.c = (lax.axis_index(a) for a in AXES)
        self.z = 2 * self.zh + self.zl
        self.inner = self.zl != self.zh
        self.outer = self.zl == self.zh
        self.to_inner = self.at_z(self.z + 1 - 2 * self.zh)
        self.to_outer = self.at_z(3 * self.zh)
        self.x_plus = [lax.rem(self.x + d, 4) for d in range(4)]
        self.y_plus = [lax.rem(self.y + d, 4) for d in range(4)]
        self.known = {}
        for key in ((1, 0, 0, 0), (-1, 0, 0, 0), (0, 1, 0, 0), (0, -1, 0, 0), (0, 0, 1, 0), (0, 0, -1, 0), (0, 0, 2, 0), (0, 0, 0, 1)):
            self.known[key] = self.place(*key)

    def at_z(self, z):
        return (self.x, lax.rem(z, 2), lax.div(z, 2), self.y, self.c)

    def step(self, dx=0, dy=0, dz=0, dc=0):
        return self.known[dx, dy, dz, dc]

    def place(self, dx, dy, dz, dc):
        z = lax.rem(self.z + dz + 4, 4)
        return (
            lax.rem(self.x + dx + 4, 4),
            lax.rem(z, 2),
            lax.div(z, 2),
            lax.rem(self.y + dy + 4, 4),
            lax.rem(self.c + dc, 2),
        )


def enter(me):
    barrier = pltpu.get_barrier_semaphore()
    steps = [
        dict(dx=1), dict(dx=-1), dict(dy=1), dict(dy=-1),
        dict(dz=1), dict(dz=-1), dict(dz=2), dict(dc=1),
    ]
    for step in steps:
        pl.semaphore_signal(barrier, inc=1, device_id=me.step(**step), device_id_type=MESH)
    pl.semaphore_wait(barrier, len(steps))


def remote(src, dst, send, recv, device):
    return pltpu.make_async_remote_copy(
        src_ref=src, dst_ref=dst, send_sem=send, recv_sem=recv, device_id=device, device_id_type=MESH
    )


def dot(left, right, left_dim, right_dim):
    return lax.dot_general(
        left, right, (((left_dim,), (right_dim,)), ((), ())), preferred_element_type=jnp.float32
    )


def gelu_slope(preact):
    cumulative = 0.5 * (1.0 + lax.erf(preact * inv_sqrt_two))
    density = jnp.exp(-0.5 * preact * preact) * inv_sqrt_two_pi
    return cumulative + preact * density


def split(value):
    high = value.astype(jnp.bfloat16)
    return high, (value - high.astype(jnp.float32)).astype(jnp.bfloat16)


def strips(count, size, body):
    def one(i, carry):
        body(pl.multiple_of(i * size, size))
        return carry

    lax.fori_loop(0, count, one, 0)


def kernel(
    inputs, wt, cot, wout, xout, xo, wf,
    wh, wl, gh, gl, dw, far, near, zin, cin, yfar, ynear, xz,
    zs, zr, fs, xs, xr, gs, gr, s1, r1, sy, ry, sf, rf, sc, rc, ls,
    pfs, pfr, pns, pnr, qs, qr, os_, cs, cr, yfs, yfr, yns, ynr, s2, r2,
):
    me = Place()
    r, half = wt.shape
    tokens = inputs.shape[0]
    rows = r // PIECES
    cols = half // PIECES
    tok = tokens // 8
    dirs = ((0, 1), (1, -1))

    def piece(p):
        return pl.ds(p * rows, rows)

    def block(p):
        return pl.ds(p * cols, cols)

    def part(y, c):
        return pl.ds((y * 2 + c) * tok, tok)

    def y_at(d):
        return me.y_plus[d % 4]

    enter(me)

    slot = me.zl + me.zh - 2 * me.zl * me.zh
    for p in range(PIECES):
        remote(wt.at[piece(p)], wf.at[0, slot, piece(p)], zs.at[p], zr.at[slot, p], me.to_inner).start()

        @pl.when(me.outer)
        def _():
            pltpu.make_async_copy(wt.at[piece(p)], wf.at[0, 0, piece(p)], zr.at[0, p]).start()

    mine = part(me.y, me.c)
    first = remote(inputs.at[mine], xo.at[mine], s1, r1, me.step(dz=2))
    first.start()

    def spread(k):
        s = slot * (k % 2) + (1 - slot) * (k // PIECES)
        p = slot * (k // 2) + (1 - slot) * (k % PIECES)
        here = wf.at[0, s, piece(p)]
        pltpu.make_async_copy(here, here, zr.at[s, p]).wait()

        @pl.when(me.inner & (s == 1))
        def _():
            remote(here, here, fs.at[p], zr.at[s, p], me.to_outer).start()

        for d, dx in dirs:
            remote(here, wf.at[1 + d, s, piece(p)], xs.at[d, s, p], xr.at[d, s, p], me.step(dx=dx)).start()

    def pass_on(p):
        for d, dx in dirs:
            there = wf.at[1 + d, d, piece(p)]
            remote(there, there, gs.at[d, p], xr.at[d, d, p], me.step(dx=dx)).wait_recv()
            remote(there, wf.at[3, d, piece(p)], gs.at[d, p], gr.at[d, p], me.step(dx=dx)).start()

    def straight(d, p):
        return remote(
            dw.at[2 - d, 1 - d, :, block(p)], near.at[d, 1 - d, :, block(p)],
            pns.at[d, 1 - d, p], pnr.at[d, 1 - d, p], me.step(dx=dirs[d][1]),
        )

    def opposite(d, p):
        return remote(
            dw.at[3, d, :, block(p)], far.at[d, :, block(p)], pfs.at[d, p], pfr.at[d, p], me.step(dx=dirs[d][1])
        )

    def onward(d, p):
        return remote(
            far.at[d, :, block(p)], near.at[d, d, :, block(p)], pns.at[d, d, p], pnr.at[d, d, p], me.step(dx=dirs[d][1])
        )

    def compute(xh, xl, stage, cstage):
        def split_inputs(source, s):
            n = 128
            loads = [
                pltpu.make_async_copy(source.at[pl.ds(i * n, n)], stage.at[i % 2, pl.ds(0, n)], ls.at[i % 2])
                for i in range(tokens // n)
            ]
            loads[0].start()
            for i in range(tokens // n):
                if i + 1 < len(loads):
                    loads[i + 1].start()
                loads[i].wait()

                def strip(at):
                    high, low = split(stage[i % 2, pl.ds(at, 16)])
                    to = pl.ds(pl.multiple_of(i * n + at, 16), 16)
                    xh[to, s * half : (s + 1) * half] = high
                    xl[to, s * half : (s + 1) * half] = low

                strips(n // 16, 16, strip)

        def split_weight(units):
            loads = [
                pltpu.make_async_copy(wf.at[j, s], stage.at[i % 2], ls.at[i % 2]) for i, (j, s) in enumerate(units)
            ]
            loads[0].start()
            for i, (j, s) in enumerate(units):
                if i + 1 < len(loads):
                    loads[i + 1].start()
                loads[i].wait()

                def strip(at):
                    high, low = split(stage[i % 2, pl.ds(at, 16)])
                    to = pl.ds(pl.multiple_of(j * r + at, 16), 16)
                    wh[to, s * half : (s + 1) * half] = high
                    wl[to, s * half : (s + 1) * half] = low

                strips(r // 16, 16, strip)

        def turn_cotangent(j):
            column = me.x_plus[(0, 3, 1, 2)[j]] * (2 * r)
            n = cstage.shape[1]
            loads = [
                pltpu.make_async_copy(
                    cot.at[pl.ds(i * n, n), pl.ds(pl.multiple_of(column, 128), 2 * r)], cstage.at[i % 2], ls.at[i % 2]
                )
                for i in range(tokens // n)
            ]
            loads[0].start()
            for i in range(len(loads)):
                if i + 1 < len(loads):
                    loads[i + 1].start()
                loads[i].wait()
                turned = cstage[i % 2].T
                dw[j, 1, :, i * n : (i + 1) * n] = jnp.where(me.zh == 0, turned[:r], turned[r:])

        def preact(j, count, s):
            of = slice(s * half, (s + 1) * half)

            def tile(at):
                to = pl.ds(at, 256)
                left = slice(j * r, (j + count) * r)
                value = (
                    dot(wh[left, of], xh[to, of], 1, 1)
                    + dot(wl[left, of], xh[to, of], 1, 1)
                    + dot(wh[left, of], xl[to, of], 1, 1)
                )
                for i in range(count):
                    new = value[i * r : (i + 1) * r]
                    dw[j + i, 0, :, to] = new if s == 0 else dw[j + i, 0, :, to] + new

            strips(tokens // 256, 256, tile)

        def pre_grad(j):
            def strip(at):
                from_ = pl.ds(at, 16)
                grad = dw[j, 1, from_, :tokens] * gelu_slope(dw[j, 0, from_, :tokens])
                to = pl.ds(pl.multiple_of(j * r + at, 16), 16)
                gh[to], gl[to] = split(grad)

            strips(r // 16, 16, strip)

        def weight_grad(j, count, s, p):
            left = slice(j * r, (j + count) * r)

            def tile(at):
                of = pl.ds(pl.multiple_of(s * half + p * cols + at, 256), 256)
                value = (
                    dot(gh[left], xh[:, of], 1, 0) + dot(gl[left], xh[:, of], 1, 0) + dot(gh[left], xl[:, of], 1, 0)
                )
                to = pl.ds(pl.multiple_of(p * cols + at, 256), 256)
                for i in range(count):
                    dw[j + i, s, :, to] = value[i * r : (i + 1) * r]

            strips(cols // 256, 256, tile)

        spread(0)
        spread(1)
        split_inputs(inputs, 0)
        spread(2)
        spread(3)
        turn_cotangent(0)
        spread(4)
        spread(5)
        first.wait_recv()
        across = [remote(xo.at[mine], xo.at[mine], sy.at[d], ry.at[d], me.step(dy=dy)) for d, dy in dirs]
        for copy in across:
            copy.start()
        shares = [remote(xo.at[mine], xo.at[mine], sc.at[0], rc.at[0], me.step(dc=1))]
        shares[0].start()
        split_weight([(0, 0), (0, 1)])
        preact(0, 1, 0)
        pass_on(0)
        turn_cotangent(1)
        halves = []
        for d, dy in dirs:
            across[d].wait_recv()
            from_y = y_at(-dy)
            rows_of = pl.ds((from_y * 2 + me.c) * tok + d * (tok // 2), tok // 2)
            halves.append(remote(xo.at[rows_of], xo.at[rows_of], sf.at[d], rf.at[d], me.step(dy=dy)))
            halves[-1].start()
            whole = part(from_y, me.c)
            shares.append(remote(xo.at[whole], xo.at[whole], sc.at[1 + d], rc.at[1 + d], me.step(dc=1)))
            shares[-1].start()
        turn_cotangent(2)
        pass_on(1)
        turn_cotangent(3)
        across_far = part(y_at(2), me.c)
        for d in range(2):
            halves[d].wait_recv()
        shares.append(remote(xo.at[across_far], xo.at[across_far], sc.at[3], rc.at[3], me.step(dc=1)))
        shares[-1].start()
        for copy in shares:
            copy.wait_recv()
        split_inputs(xo, 1)
        pass_on(2)
        for d in range(2):
            for p in range(PIECES):
                unit = wf.at[1 + d, 1 - d, piece(p)]
                remote(unit, unit, xs.at[d, 1 - d, p], xr.at[d, 1 - d, p], me.step(dc=1)).wait_recv()
        split_weight([(1, 0), (1, 1), (2, 0), (2, 1)])
        preact(0, 1, 1)
        pre_grad(0)
        preact(1, 2, 0)
        preact(1, 2, 1)
        pre_grad(1)
        pre_grad(2)
        for p in range(PIECES):
            for d, step in dirs:
                weight_grad(2 - d, 1, 1 - d, p)
                straight(d, p).start()
        for d in range(2):
            for p in range(PIECES):
                unit = wf.at[3, d, piece(p)]
                remote(unit, unit, gs.at[d, p], gr.at[d, p], me.step(dc=1)).wait_recv()
        split_weight([(3, 0), (3, 1)])
        preact(3, 1, 0)
        preact(3, 1, 1)
        pre_grad(3)
        for p in range(PIECES):
            for d, step in dirs:
                weight_grad(3, 1, d, p)
                opposite(d, p).start()
        for p in range(PIECES):
            for d, step in dirs:
                weight_grad(2 - d, 1, d, p)
        for p in range(PIECES):
            for s in range(2):
                weight_grad(0, 1, s, p)
        for p in range(PIECES):
            remote(wt.at[piece(p)], wt.at[piece(p)], zs.at[p], zs.at[p], me.step(dc=1)).wait_send()

            @pl.when(me.inner)
            def _():
                remote(wt.at[piece(p)], wt.at[piece(p)], fs.at[p], fs.at[p], me.step(dc=1)).wait_send()

            for d in range(2):
                for s in range(2):
                    remote(wt.at[piece(p)], wt.at[piece(p)], xs.at[d, s, p], xs.at[d, s, p], me.step(dc=1)).wait_send()
                remote(wt.at[piece(p)], wt.at[piece(p)], gs.at[d, p], gs.at[d, p], me.step(dc=1)).wait_send()
        for copy in across + halves + shares + [first]:
            copy.wait_send()

    f32, bf16 = jnp.float32, jnp.bfloat16
    pl.run_scoped(
        compute,
        pltpu.VMEM((tokens, 2 * half), bf16), pltpu.VMEM((tokens, 2 * half), bf16),
        pltpu.VMEM((2, r, half), f32), pltpu.VMEM((2, 256, 2 * r), f32),
    )

    def sums(acc):
        order = [(s, dy) for s in (1, 0) for dy in (2, 1, -1, 0)]
        shares = []
        y_copies = {}
        left = pl.ds(0, tokens // 2)
        right = pl.ds(tokens // 2, tokens // 2)
        side = (left, right)
        own = pl.ds(pl.multiple_of(me.c * r, r), r)
        others = pl.ds(pl.multiple_of((1 - me.c) * r, r), r)

        def input_grad(i):
            s, dy = order[i]
            of = pl.ds(pl.multiple_of(s * half + y_at(dy) * (2 * r), 128), 2 * r)
            acc[i] = dot(wh[:, of], gh[...], 0, 0) + dot(wl[:, of], gh[...], 0, 0) + dot(wh[:, of], gl[...], 0, 0)
            copy = remote(acc.at[i, others], cin.at[i], cs.at[i], cr.at[i], me.step(dc=1))
            copy.start()
            shares.append(copy)

        def on_chip(i):
            shares[i].wait_recv()
            acc[i, own] = acc[i, own] + cin[i]

        def y_start(i, d, kind, source, target, sems):
            copy = remote(source, target, sems[0], sems[1], me.step(dy=dirs[d][1]))
            copy.start()
            y_copies[i, d, kind] = copy

        def y_far(s):
            i = 4 * (1 - s)
            on_chip(i)
            for d in range(2):
                y_start(s, d, 0, acc.at[i, own, side[d]], yfar.at[s, d], (yfs.at[s, d], yfr.at[s, d]))

        def y_straight(s, d):
            i = 4 * (1 - s) + 1 + d
            on_chip(i)
            o = 1 - d
            y_start(s, d, 1, acc.at[i, own, side[o]], ynear.at[s, d, :, side[o]], (yns.at[s, d, o], ynr.at[s, d, o]))

        def y_pass(s):
            for d in range(2):
                i = 4 * (1 - s) + 1 + d
                y_copies[s, d, 0].wait_recv()
                yfar[s, d] = yfar[s, d] + acc[i, own, side[d]]
                y_start(s, d, 2, yfar.at[s, d], ynear.at[s, d, :, side[d]], (yns.at[s, d, d], ynr.at[s, d, d]))

        def y_sum(s):
            i = 4 * (1 - s) + 3
            for d in range(2):
                y_copies[s, d, 1].wait_recv()
                y_copies[s, d, 2].wait_recv()
            acc[i, own] = acc[i, own] + ynear[s, 0] + ynear[s, 1]

        def x_pass(p):
            for d, step in dirs:
                opposite(d, p).wait_recv()
                far[d, :, block(p)] = far[d, :, block(p)] + dw[2 - d, d, :, block(p)]
                onward(d, p).start()

        input_grad(0)
        input_grad(1)
        y_far(1)
        input_grad(2)
        y_straight(1, 0)
        input_grad(3)
        y_straight(1, 1)
        input_grad(4)
        on_chip(3)
        input_grad(5)
        y_far(0)
        input_grad(6)
        y_straight(0, 0)
        input_grad(7)
        y_straight(0, 1)
        on_chip(7)
        y_pass(1)
        x_pass(0)
        x_pass(1)
        y_pass(0)
        x_pass(2)
        y_sum(1)
        last = remote(acc.at[3, own], xz, s2, r2, me.step(dz=2))
        last.start()

        for p in range(PIECES):
            for d in range(2):
                straight(d, p).wait_recv()
                onward(d, p).wait_recv()
            for s in range(2):
                dw[0, s, :, block(p)] = dw[0, s, :, block(p)] + near[0, s, :, block(p)] + near[1, s, :, block(p)]

            @pl.when(me.outer)
            def _():
                remote(dw.at[0, 1, :, block(p)], zin.at[0, :, block(p)], qs.at[p], qr.at[0, p], me.to_inner).start()

            @pl.when(me.inner)
            def _():
                remote(dw.at[0, 0, :, block(p)], zin.at[1, :, block(p)], qs.at[p], qr.at[1, p], me.to_outer).start()

        y_sum(0)
        for p in range(PIECES):
            @pl.when(me.inner)
            def _():
                here = zin.at[0, :, block(p)]
                remote(here, here, os_.at[p], qr.at[0, p], me.to_inner).wait_recv()
                zin[0, :, block(p)] = dw[0, 1, :, block(p)] + zin[0, :, block(p)]
                remote(here, zin.at[1, :, block(p)], os_.at[p], qr.at[1, p], me.to_inner).start()

        last.wait_recv()
        acc[7, own] = acc[7, own] + xz[...]
        x_out = pltpu.make_async_copy(acc.at[7, own], xout, ls.at[0])
        x_out.start()
        for p in range(PIECES):
            here = zin.at[1, :, block(p)]
            remote(here, here, qs.at[p], qr.at[1, p], me.step(dz=1)).wait_recv()

            @pl.when(me.outer)
            def _():
                zin[1, :, block(p)] = dw[0, 0, :, block(p)] + zin[1, :, block(p)]

        w_out = pltpu.make_async_copy(zin.at[1], wout, ls.at[1])
        w_out.start()

        for p in range(PIECES):
            here = zin.at[1, :, block(p)]
            remote(here, here, qs.at[p], qr.at[1, p], me.step(dz=1)).wait_send()

            @pl.when(me.inner)
            def _():
                remote(here, here, os_.at[p], qr.at[0, p], me.step(dz=1)).wait_send()

        for p in range(PIECES):
            for d in range(2):
                for copy in (opposite(d, p), straight(d, p), onward(d, p)):
                    copy.wait_send()
        for copy in list(y_copies.values()) + shares + [last]:
            copy.wait_send()
        x_out.wait()
        w_out.wait()

    pl.run_scoped(sums, pltpu.VMEM((8, 2 * r, tokens), f32))


def fused(inputs, wt, cot):
    dma = pltpu.SemaphoreType.DMA
    vmem = pltpu.VMEM
    f32, bf16 = jnp.float32, jnp.bfloat16
    r, d = wt.shape
    t = inputs.shape[0]
    hbm = pl.BlockSpec(memory_space=pltpu.HBM)
    n = PIECES
    return pl.pallas_call(
        kernel,
        out_shape=(
            jax.ShapeDtypeStruct((r, d), f32),
            jax.ShapeDtypeStruct((r, t), f32),
            jax.ShapeDtypeStruct((t, d), f32),
            jax.ShapeDtypeStruct((4, 2, r, d), f32),
        ),
        in_specs=[hbm] * 3,
        out_specs=(hbm,) * 4,
        scratch_shapes=[
            vmem((4 * r, 2 * d), bf16), vmem((4 * r, 2 * d), bf16), vmem((4 * r, t), bf16), vmem((4 * r, t), bf16),
            vmem((4, 2, r, d), f32), vmem((2, r, d), f32), vmem((2, 2, r, d), f32), vmem((2, r, d), f32),
            vmem((8, r, t), f32), vmem((2, 2, r, t // 2), f32), vmem((2, 2, r, t), f32), vmem((r, t), f32),
            dma((n,)), dma((2, n)), dma((n,)), dma((2, 2, n)), dma((2, 2, n)), dma((2, n)), dma((2, n)),
            dma, dma, dma((2,)), dma((2,)), dma((2,)), dma((2,)), dma((4,)), dma((4,)), dma((2,)),
            dma((2, n)), dma((2, n)), dma((2, 2, n)), dma((2, 2, n)), dma((n,)), dma((2, n)), dma((n,)),
            dma((8,)), dma((8,)), dma((2, 2)), dma((2, 2)), dma((2, 2, 2)), dma((2, 2, 2)), dma, dma,
        ],
        compiler_params=pltpu.CompilerParams(collective_id=0, has_side_effects=True, vmem_limit_bytes=60 << 20),
    )(inputs, wt, cot)[:2]


def local(inputs, weight, cotangent):
    wout, xout = fused(inputs, weight.T, cotangent)
    return (xout.T, wout.T)


def solution(mesh):
    torus = Mesh(mesh.devices.reshape(4, 2, 2, 4, 2), AXES)
    in_specs = (P(("x", "zl"), "zh"), P("zh", ("y", "c", "x", "zl")), P(("x", "zl"), ("y", "c")))
    out_specs = (P(("x", "zl"), ("zh", "y", "c")), P("zh", ("y", "c", "x", "zl")))
    return jax.shard_map(local, mesh=torus, in_specs=in_specs, out_specs=out_specs, check_vma=False)
```

```python
import jax
import jax.numpy as jnp
from jax import lax
from jax.experimental import pallas as pl
from jax.experimental.pallas import tpu as pltpu
from jax.sharding import Mesh
from jax.sharding import PartitionSpec as P

AXES = ("x", "zl", "zh", "y", "c")
MESH = pl.DeviceIdType.MESH
PIECES = 6

inv_sqrt_two = 0.7071067811865476
inv_sqrt_two_pi = 0.3989422804014327


class Place:
    def __init__(self):
        self.x, self.zl, self.zh, self.y, self.c = (lax.axis_index(a) for a in AXES)
        self.z = 2 * self.zh + self.zl
        self.inner = self.zl != self.zh
        self.outer = self.zl == self.zh
        self.to_inner = self.at_z(self.z + 1 - 2 * self.zh)
        self.to_outer = self.at_z(3 * self.zh)
        self.x_plus = [lax.rem(self.x + d, 4) for d in range(4)]
        self.y_plus = [lax.rem(self.y + d, 4) for d in range(4)]
        self.known = {}
        for key in ((1, 0, 0, 0), (-1, 0, 0, 0), (0, 1, 0, 0), (0, -1, 0, 0), (0, 0, 1, 0), (0, 0, -1, 0), (0, 0, 2, 0), (0, 0, 0, 1)):
            self.known[key] = self.place(*key)

    def at_z(self, z):
        return (self.x, lax.rem(z, 2), lax.div(z, 2), self.y, self.c)

    def step(self, dx=0, dy=0, dz=0, dc=0):
        return self.known[dx, dy, dz, dc]

    def place(self, dx, dy, dz, dc):
        z = lax.rem(self.z + dz + 4, 4)
        return (
            lax.rem(self.x + dx + 4, 4),
            lax.rem(z, 2),
            lax.div(z, 2),
            lax.rem(self.y + dy + 4, 4),
            lax.rem(self.c + dc, 2),
        )


def enter(me):
    barrier = pltpu.get_barrier_semaphore()
    steps = [
        dict(dx=1), dict(dx=-1), dict(dy=1), dict(dy=-1),
        dict(dz=1), dict(dz=-1), dict(dz=2), dict(dc=1),
    ]
    for step in steps:
        pl.semaphore_signal(barrier, inc=1, device_id=me.step(**step), device_id_type=MESH)
    pl.semaphore_wait(barrier, len(steps))


def remote(src, dst, send, recv, device):
    return pltpu.make_async_remote_copy(
        src_ref=src, dst_ref=dst, send_sem=send, recv_sem=recv, device_id=device, device_id_type=MESH
    )


def dot(left, right, left_dim, right_dim):
    return lax.dot_general(
        left, right, (((left_dim,), (right_dim,)), ((), ())), preferred_element_type=jnp.float32
    )


def gelu_slope(preact):
    cumulative = 0.5 * (1.0 + lax.erf(preact * inv_sqrt_two))
    density = jnp.exp(-0.5 * preact * preact) * inv_sqrt_two_pi
    return cumulative + preact * density


def split(value):
    high = value.astype(jnp.bfloat16)
    return high, (value - high.astype(jnp.float32)).astype(jnp.bfloat16)


def strips(count, size, body):
    def one(i, carry):
        body(pl.multiple_of(i * size, size))
        return carry

    lax.fori_loop(0, count, one, 0)


def kernel(
    inputs, wt, cot, wout, xout, xo, wf,
    wh, wl, gh, gl, dw, far, near, zin, cin, yfar, ynear, xz,
    zs, zr, fs, xs, xr, gs, gr, s1, r1, sy, ry, sf, rf, sc, rc, ls,
    pfs, pfr, pns, pnr, qs, qr, os_, cs, cr, yfs, yfr, yns, ynr, s2, r2,
):
    me = Place()
    r, half = wt.shape
    tokens = inputs.shape[0]
    rows = r // PIECES
    cols = half // PIECES
    tok = tokens // 8
    dirs = ((0, 1), (1, -1))

    def piece(p):
        return pl.ds(p * rows, rows)

    def block(p):
        return pl.ds(p * cols, cols)

    def y_at(d):
        return me.y_plus[d % 4]

    enter(me)

    slot = me.zl + me.zh - 2 * me.zl * me.zh
    def send_unit(p):
        remote(wt.at[piece(p)], wf.at[0, slot, piece(p)], zs.at[p], zr.at[slot, p], me.to_inner).start()

        @pl.when(me.outer)
        def _():
            pltpu.make_async_copy(wt.at[piece(p)], wf.at[0, 0, piece(p)], zr.at[0, p]).start()

    step_rows = tok // 2

    def rows_of(y, h):
        return pl.ds((y * 2 + me.c) * tok + h * step_rows, step_rows)

    def fetch(h):
        at = rows_of(me.y, h)
        return remote(inputs.at[at], xo.at[at], s1.at[h], r1.at[h], me.step(dz=2))

    def across(h, d):
        at = rows_of(me.y, h)
        return remote(xo.at[at], xo.at[at], sy.at[h, d], ry.at[h, d], me.step(dy=dirs[d][1]))

    def onto(h, d):
        at = pl.ds((y_at(-dirs[d][1]) * 2 + me.c) * tok + h * step_rows + d * (step_rows // 2), step_rows // 2)
        return remote(xo.at[at], xo.at[at], sf.at[h, d], rf.at[h, d], me.step(dy=dirs[d][1]))

    def share(h, k):
        at = rows_of(y_at((0, -1, 1, 2)[k]), h)
        return remote(xo.at[at], xo.at[at], sc.at[h, k], rc.at[h, k], me.step(dc=1))

    for h in range(2):
        send_unit(3 * h)
        send_unit(3 * h + 1)
        fetch(h).start()
        send_unit(3 * h + 2)

    def spread(k):
        s = slot * (k % 2) + (1 - slot) * (k // PIECES)
        p = slot * (k // 2) + (1 - slot) * (k % PIECES)
        here = wf.at[0, s, piece(p)]
        pltpu.make_async_copy(here, here, zr.at[s, p]).wait()

        @pl.when(me.inner & (s == 1))
        def _():
            remote(here, here, fs.at[p], zr.at[s, p], me.to_outer).start()

        for d, dx in dirs:
            remote(here, wf.at[1 + d, s, piece(p)], xs.at[d, s, p], xr.at[d, s, p], me.step(dx=dx)).start()

    def pass_on(p):
        for d, dx in dirs:
            there = wf.at[1 + d, d, piece(p)]
            remote(there, there, gs.at[d, p], xr.at[d, d, p], me.step(dx=dx)).wait_recv()
            remote(there, wf.at[3, d, piece(p)], gs.at[d, p], gr.at[d, p], me.step(dx=dx)).start()

    def straight(d, p):
        return remote(
            dw.at[2 - d, 1 - d, :, block(p)], near.at[d, 1 - d, :, block(p)],
            pns.at[d, 1 - d, p], pnr.at[d, 1 - d, p], me.step(dx=dirs[d][1]),
        )

    def opposite(d, p):
        return remote(
            dw.at[3, d, :, block(p)], far.at[d, :, block(p)], pfs.at[d, p], pfr.at[d, p], me.step(dx=dirs[d][1])
        )

    def onward(d, p):
        return remote(
            far.at[d, :, block(p)], near.at[d, d, :, block(p)], pns.at[d, d, p], pnr.at[d, d, p], me.step(dx=dirs[d][1])
        )

    def compute(xh, xl, stage, cstage):
        def split_inputs(source, s):
            n = 128
            loads = [
                pltpu.make_async_copy(source.at[pl.ds(i * n, n)], stage.at[i % 2, pl.ds(0, n)], ls.at[i % 2])
                for i in range(tokens // n)
            ]
            loads[0].start()
            for i in range(tokens // n):
                if i + 1 < len(loads):
                    loads[i + 1].start()
                loads[i].wait()

                def strip(at):
                    high, low = split(stage[i % 2, pl.ds(at, 16)])
                    to = pl.ds(pl.multiple_of(i * n + at, 16), 16)
                    xh[to, s * half : (s + 1) * half] = high
                    xl[to, s * half : (s + 1) * half] = low

                strips(n // 16, 16, strip)

        def split_weight(units):
            loads = [
                pltpu.make_async_copy(wf.at[j, s], stage.at[i % 2], ls.at[i % 2]) for i, (j, s) in enumerate(units)
            ]
            loads[0].start()
            for i, (j, s) in enumerate(units):
                if i + 1 < len(loads):
                    loads[i + 1].start()
                loads[i].wait()

                def strip(at):
                    high, low = split(stage[i % 2, pl.ds(at, 16)])
                    to = pl.ds(pl.multiple_of(j * r + at, 16), 16)
                    wh[to, s * half : (s + 1) * half] = high
                    wl[to, s * half : (s + 1) * half] = low

                strips(r // 16, 16, strip)

        def turn_cotangent(j):
            column = me.x_plus[(0, 3, 1, 2)[j]] * (2 * r)
            n = cstage.shape[1]
            loads = [
                pltpu.make_async_copy(
                    cot.at[pl.ds(i * n, n), pl.ds(pl.multiple_of(column, 128), 2 * r)], cstage.at[i % 2], ls.at[i % 2]
                )
                for i in range(tokens // n)
            ]
            loads[0].start()
            for i in range(len(loads)):
                if i + 1 < len(loads):
                    loads[i + 1].start()
                loads[i].wait()
                turned = cstage[i % 2].T
                dw[j, 1, :, i * n : (i + 1) * n] = jnp.where(me.zh == 0, turned[:r], turned[r:])

        def preact(j, count, s):
            of = slice(s * half, (s + 1) * half)

            def tile(at):
                to = pl.ds(at, 256)
                left = slice(j * r, (j + count) * r)
                value = (
                    dot(wh[left, of], xh[to, of], 1, 1)
                    + dot(wl[left, of], xh[to, of], 1, 1)
                    + dot(wh[left, of], xl[to, of], 1, 1)
                )
                for i in range(count):
                    new = value[i * r : (i + 1) * r]
                    dw[j + i, 0, :, to] = new if s == 0 else dw[j + i, 0, :, to] + new

            strips(tokens // 256, 256, tile)

        def pre_grad(j):
            def strip(at):
                from_ = pl.ds(at, 16)
                grad = dw[j, 1, from_, :tokens] * gelu_slope(dw[j, 0, from_, :tokens])
                to = pl.ds(pl.multiple_of(j * r + at, 16), 16)
                gh[to], gl[to] = split(grad)

            strips(r // 16, 16, strip)

        def weight_grad(j, count, s, first, tiles):
            left = slice(j * r, (j + count) * r)
            wide = 2 * cols

            def tile(at):
                to = pl.ds(pl.multiple_of(first * wide + at, wide), wide)
                of = pl.ds(pl.multiple_of(s * half + first * wide + at, wide), wide)
                value = (
                    dot(gh[left], xh[:, of], 1, 0) + dot(gl[left], xh[:, of], 1, 0) + dot(gh[left], xl[:, of], 1, 0)
                )
                for i in range(count):
                    dw[j + i, s, :, to] = value[i * r : (i + 1) * r]

            strips(tiles, wide, tile)

        def fetched(h):
            fetch(h).wait_recv()
            for d in range(2):
                across(h, d).start()
            share(h, 0).start()

        def crossed(h):
            for d in range(2):
                across(h, d).wait_recv()
                onto(h, d).start()
                share(h, 1 + d).start()

        def met(h):
            for d in range(2):
                onto(h, d).wait_recv()
            share(h, 3).start()

        for k in range(4):
            spread(k)
        split_inputs(inputs, 0)
        fetched(0)
        for k in range(4, 8):
            spread(k)
        turn_cotangent(0)
        turn_cotangent(1)
        crossed(0)
        fetched(1)
        turn_cotangent(2)
        met(0)
        for k in range(8, 12):
            spread(k)
        turn_cotangent(3)
        pass_on(0)
        split_weight([(0, 0), (0, 1)])
        crossed(1)
        preact(0, 1, 0)
        pass_on(1)
        met(1)
        pass_on(2)
        for h in range(2):
            for k in range(4):
                share(h, k).wait_recv()
        split_inputs(xo, 1)
        preact(0, 1, 1)
        pre_grad(0)
        pass_on(3)
        weight_grad(0, 1, 0, 0, 3)
        pass_on(4)
        weight_grad(0, 1, 1, 0, 3)
        pass_on(5)
        for d in range(2):
            for p in range(PIECES):
                unit = wf.at[1 + d, 1 - d, piece(p)]
                remote(unit, unit, xs.at[d, 1 - d, p], xr.at[d, 1 - d, p], me.step(dc=1)).wait_recv()
        split_weight([(1, 0), (1, 1), (2, 0), (2, 1)])
        preact(1, 2, 0)
        preact(1, 2, 1)
        pre_grad(1)
        pre_grad(2)
        for p in range(PIECES // 2):
            for d in range(2):
                weight_grad(2 - d, 1, 1 - d, p, 1)
                straight(d, 2 * p).start()
                straight(d, 2 * p + 1).start()
        for d in range(2):
            weight_grad(2 - d, 1, d, 0, 3)
        for d in range(2):
            for p in range(PIECES):
                unit = wf.at[3, d, piece(p)]
                remote(unit, unit, gs.at[d, p], gr.at[d, p], me.step(dc=1)).wait_recv()
        split_weight([(3, 0), (3, 1)])
        preact(3, 1, 0)
        preact(3, 1, 1)
        pre_grad(3)
        for p in range(PIECES // 2):
            for d in range(2):
                weight_grad(3, 1, d, p, 1)
                opposite(d, 2 * p).start()
                opposite(d, 2 * p + 1).start()

    f32, bf16 = jnp.float32, jnp.bfloat16
    pl.run_scoped(
        compute,
        pltpu.VMEM((tokens, 2 * half), bf16), pltpu.VMEM((tokens, 2 * half), bf16),
        pltpu.VMEM((2, r, half), f32), pltpu.VMEM((2, 256, 2 * r), f32),
    )

    def sums(acc):
        order = [(s, dy) for s in (1, 0) for dy in (2, 1, -1, 0)]
        shares = []
        y_copies = {}
        left = pl.ds(0, tokens // 2)
        right = pl.ds(tokens // 2, tokens // 2)
        side = (left, right)
        own = pl.ds(pl.multiple_of(me.c * r, r), r)
        others = pl.ds(pl.multiple_of((1 - me.c) * r, r), r)

        def input_grad(i):
            s, dy = order[i]
            of = pl.ds(pl.multiple_of(s * half + y_at(dy) * (2 * r), 128), 2 * r)
            acc[i] = dot(wh[:, of], gh[...], 0, 0) + dot(wl[:, of], gh[...], 0, 0) + dot(wh[:, of], gl[...], 0, 0)
            copy = remote(acc.at[i, others], cin.at[i], cs.at[i], cr.at[i], me.step(dc=1))
            copy.start()
            shares.append(copy)

        def on_chip(i):
            shares[i].wait_recv()
            acc[i, own] = acc[i, own] + cin[i]

        def y_start(i, d, kind, source, target, sems):
            copy = remote(source, target, sems[0], sems[1], me.step(dy=dirs[d][1]))
            copy.start()
            y_copies[i, d, kind] = copy

        def y_far(s):
            i = 4 * (1 - s)
            on_chip(i)
            for d in range(2):
                y_start(s, d, 0, acc.at[i, own, side[d]], yfar.at[s, d], (yfs.at[s, d], yfr.at[s, d]))

        def y_straight(s, d):
            i = 4 * (1 - s) + 1 + d
            on_chip(i)
            o = 1 - d
            y_start(s, d, 1, acc.at[i, own, side[o]], ynear.at[s, d, :, side[o]], (yns.at[s, d, o], ynr.at[s, d, o]))

        def y_pass(s):
            for d in range(2):
                i = 4 * (1 - s) + 1 + d
                y_copies[s, d, 0].wait_recv()
                yfar[s, d] = yfar[s, d] + acc[i, own, side[d]]
                y_start(s, d, 2, yfar.at[s, d], ynear.at[s, d, :, side[d]], (yns.at[s, d, d], ynr.at[s, d, d]))

        def y_sum(s):
            i = 4 * (1 - s) + 3
            for d in range(2):
                y_copies[s, d, 1].wait_recv()
                y_copies[s, d, 2].wait_recv()
            acc[i, own] = acc[i, own] + ynear[s, 0] + ynear[s, 1]

        def x_pass(p):
            for d, step in dirs:
                opposite(d, p).wait_recv()
                far[d, :, block(p)] = far[d, :, block(p)] + dw[2 - d, d, :, block(p)]
                onward(d, p).start()

        input_grad(0)
        input_grad(1)
        y_far(1)
        input_grad(2)
        y_straight(1, 0)
        input_grad(3)
        y_straight(1, 1)
        input_grad(4)
        on_chip(3)
        input_grad(5)
        y_far(0)
        input_grad(6)
        y_straight(0, 0)
        input_grad(7)
        y_straight(0, 1)
        on_chip(7)
        x_pass(0)
        x_pass(1)
        y_pass(1)
        x_pass(2)
        x_pass(3)
        y_pass(0)
        x_pass(4)
        x_pass(5)
        last = remote(acc.at[3, own], xz, s2, r2, me.step(dz=2))

        def x_sum(p):
            for d in range(2):
                straight(d, p).wait_recv()
                onward(d, p).wait_recv()
            for s in range(2):
                dw[0, s, :, block(p)] = dw[0, s, :, block(p)] + near[0, s, :, block(p)] + near[1, s, :, block(p)]

            @pl.when(me.outer)
            def _():
                remote(dw.at[0, 1, :, block(p)], zin.at[0, :, block(p)], qs.at[p], qr.at[0, p], me.to_inner).start()

            @pl.when(me.inner)
            def _():
                remote(dw.at[0, 0, :, block(p)], zin.at[1, :, block(p)], qs.at[p], qr.at[1, p], me.to_outer).start()

        def z_pass(p):
            @pl.when(me.inner)
            def _():
                here = zin.at[0, :, block(p)]
                remote(here, here, os_.at[p], qr.at[0, p], me.to_inner).wait_recv()
                zin[0, :, block(p)] = dw[0, 1, :, block(p)] + zin[0, :, block(p)]
                remote(here, zin.at[1, :, block(p)], os_.at[p], qr.at[1, p], me.to_inner).start()

        for p in range(PIECES):
            x_sum(p)
            if p > 0:
                z_pass(p - 1)
            if p == 3:
                y_sum(1)
                last.start()
        z_pass(PIECES - 1)
        y_sum(0)
        last.wait_recv()
        acc[7, own] = acc[7, own] + xz[...]
        x_out = pltpu.make_async_copy(acc.at[7, own], xout, ls.at[0])
        x_out.start()
        for p in range(PIECES):
            here = zin.at[1, :, block(p)]
            remote(here, here, qs.at[p], qr.at[1, p], me.step(dz=1)).wait_recv()

            @pl.when(me.outer)
            def _():
                zin[1, :, block(p)] = dw[0, 0, :, block(p)] + zin[1, :, block(p)]

        w_out = pltpu.make_async_copy(zin.at[1], wout, ls.at[1])
        w_out.start()

        for p in range(PIECES):
            here = zin.at[1, :, block(p)]
            remote(here, here, qs.at[p], qr.at[1, p], me.step(dz=1)).wait_send()

            @pl.when(me.inner)
            def _():
                remote(here, here, os_.at[p], qr.at[0, p], me.step(dz=1)).wait_send()

        for p in range(PIECES):
            for d in range(2):
                for copy in (opposite(d, p), straight(d, p), onward(d, p)):
                    copy.wait_send()
            unit = wt.at[piece(p)]
            remote(unit, unit, zs.at[p], zs.at[p], me.step(dc=1)).wait_send()

            @pl.when(me.inner)
            def _():
                remote(unit, unit, fs.at[p], fs.at[p], me.step(dc=1)).wait_send()

            for d in range(2):
                for s in range(2):
                    remote(unit, unit, xs.at[d, s, p], xs.at[d, s, p], me.step(dc=1)).wait_send()
                remote(unit, unit, gs.at[d, p], gs.at[d, p], me.step(dc=1)).wait_send()
        for h in range(2):
            fetch(h).wait_send()
            for d in range(2):
                across(h, d).wait_send()
                onto(h, d).wait_send()
            for k in range(4):
                share(h, k).wait_send()
        for copy in list(y_copies.values()) + shares + [last]:
            copy.wait_send()
        x_out.wait()
        w_out.wait()

    pl.run_scoped(sums, pltpu.VMEM((8, 2 * r, tokens), f32))


def fused(inputs, wt, cot):
    dma = pltpu.SemaphoreType.DMA
    vmem = pltpu.VMEM
    f32, bf16 = jnp.float32, jnp.bfloat16
    r, d = wt.shape
    t = inputs.shape[0]
    hbm = pl.BlockSpec(memory_space=pltpu.HBM)
    n = PIECES
    return pl.pallas_call(
        kernel,
        out_shape=(
            jax.ShapeDtypeStruct((r, d), f32),
            jax.ShapeDtypeStruct((r, t), f32),
            jax.ShapeDtypeStruct((t, d), f32),
            jax.ShapeDtypeStruct((4, 2, r, d), f32),
        ),
        in_specs=[hbm] * 3,
        out_specs=(hbm,) * 4,
        scratch_shapes=[
            vmem((4 * r, 2 * d), bf16), vmem((4 * r, 2 * d), bf16), vmem((4 * r, t), bf16), vmem((4 * r, t), bf16),
            vmem((4, 2, r, d), f32), vmem((2, r, d), f32), vmem((2, 2, r, d), f32), vmem((2, r, d), f32),
            vmem((8, r, t), f32), vmem((2, 2, r, t // 2), f32), vmem((2, 2, r, t), f32), vmem((r, t), f32),
            dma((n,)), dma((2, n)), dma((n,)), dma((2, 2, n)), dma((2, 2, n)), dma((2, n)), dma((2, n)),
            dma((2,)), dma((2,)), dma((2, 2)), dma((2, 2)), dma((2, 2)), dma((2, 2)), dma((2, 4)), dma((2, 4)), dma((2,)),
            dma((2, n)), dma((2, n)), dma((2, 2, n)), dma((2, 2, n)), dma((n,)), dma((2, n)), dma((n,)),
            dma((8,)), dma((8,)), dma((2, 2)), dma((2, 2)), dma((2, 2, 2)), dma((2, 2, 2)), dma, dma,
        ],
        compiler_params=pltpu.CompilerParams(collective_id=0, has_side_effects=True, vmem_limit_bytes=60 << 20),
    )(inputs, wt, cot)[:2]


def local(inputs, weight, cotangent):
    wout, xout = fused(inputs, weight.T, cotangent)
    return (xout.T, wout.T)


def solution(mesh):
    torus = Mesh(mesh.devices.reshape(4, 2, 2, 4, 2), AXES)
    in_specs = (P(("x", "zl"), "zh"), P("zh", ("y", "c", "x", "zl")), P(("x", "zl"), ("y", "c")))
    out_specs = (P(("x", "zl"), ("zh", "y", "c")), P("zh", ("y", "c", "x", "zl")))
    return jax.shard_map(local, mesh=torus, in_specs=in_specs, out_specs=out_specs, check_vma=False)
```

```python
import jax
import jax.numpy as jnp
from jax import lax
from jax.experimental import pallas as pl
from jax.experimental.pallas import tpu as pltpu
from jax.sharding import Mesh
from jax.sharding import PartitionSpec as P

AXES = ("x", "zl", "zh", "y", "c")
MESH = pl.DeviceIdType.MESH
PIECES = 6
EARLY = 4

inv_sqrt_two = 0.7071067811865476
inv_sqrt_two_pi = 0.3989422804014327


class Place:
    def __init__(self):
        self.x, self.zl, self.zh, self.y, self.c = (lax.axis_index(a) for a in AXES)
        self.z = 2 * self.zh + self.zl
        self.inner = self.zl != self.zh
        self.outer = self.zl == self.zh
        self.to_inner = self.at_z(self.z + 1 - 2 * self.zh)
        self.to_outer = self.at_z(3 * self.zh)
        self.x_plus = [lax.rem(self.x + d, 4) for d in range(4)]
        self.y_plus = [lax.rem(self.y + d, 4) for d in range(4)]
        self.known = {}
        for key in ((1, 0, 0, 0), (-1, 0, 0, 0), (0, 1, 0, 0), (0, -1, 0, 0), (0, 0, 1, 0), (0, 0, -1, 0), (0, 0, 2, 0), (0, 0, 0, 1)):
            self.known[key] = self.place(*key)

    def at_z(self, z):
        return (self.x, lax.rem(z, 2), lax.div(z, 2), self.y, self.c)

    def step(self, dx=0, dy=0, dz=0, dc=0):
        return self.known[dx, dy, dz, dc]

    def place(self, dx, dy, dz, dc):
        z = lax.rem(self.z + dz + 4, 4)
        return (
            lax.rem(self.x + dx + 4, 4),
            lax.rem(z, 2),
            lax.div(z, 2),
            lax.rem(self.y + dy + 4, 4),
            lax.rem(self.c + dc, 2),
        )


def enter(me):
    barrier = pltpu.get_barrier_semaphore()
    steps = [
        dict(dx=1), dict(dx=-1), dict(dy=1), dict(dy=-1),
        dict(dz=1), dict(dz=-1), dict(dz=2), dict(dc=1),
    ]
    for step in steps:
        pl.semaphore_signal(barrier, inc=1, device_id=me.step(**step), device_id_type=MESH)
    pl.semaphore_wait(barrier, len(steps))


def remote(src, dst, send, recv, device):
    return pltpu.make_async_remote_copy(
        src_ref=src, dst_ref=dst, send_sem=send, recv_sem=recv, device_id=device, device_id_type=MESH
    )


def dot(left, right, left_dim, right_dim):
    return lax.dot_general(
        left, right, (((left_dim,), (right_dim,)), ((), ())), preferred_element_type=jnp.float32
    )


def gelu_slope(preact):
    cumulative = 0.5 * (1.0 + lax.erf(preact * inv_sqrt_two))
    density = jnp.exp(-0.5 * preact * preact) * inv_sqrt_two_pi
    return cumulative + preact * density


def split(value):
    high = value.astype(jnp.bfloat16)
    return high, (value - high.astype(jnp.float32)).astype(jnp.bfloat16)


def strips(count, size, body):
    def one(i, carry):
        body(pl.multiple_of(i * size, size))
        return carry

    lax.fori_loop(0, count, one, 0)


def kernel(
    inputs, wt, cot, wout, xout, xo, wf,
    wh, wl, gh, gl, dw, far, near, zin, cin, yfar, ynear, xz,
    zs, zr, fs, xs, xr, gs, gr, s1, r1, sy, ry, sf, rf, sc, rc, ls,
    pfs, pfr, pns, pnr, qs, qr, os_, cs, cr, yfs, yfr, yns, ynr, s2, r2,
):
    me = Place()
    r, half = wt.shape
    tokens = inputs.shape[0]
    rows = r // PIECES
    cols = half // PIECES
    tok = tokens // 8
    dirs = ((0, 1), (1, -1))

    def piece(p):
        return pl.ds(p * rows, rows)

    def block(p):
        return pl.ds(p * cols, cols)

    def y_at(d):
        return me.y_plus[d % 4]

    enter(me)

    slot = me.zl + me.zh - 2 * me.zl * me.zh
    def send_unit(p):
        remote(wt.at[piece(p)], wf.at[0, slot, piece(p)], zs.at[p], zr.at[slot, p], me.to_inner).start()

        @pl.when(me.outer)
        def _():
            pltpu.make_async_copy(wt.at[piece(p)], wf.at[0, 0, piece(p)], zr.at[0, p]).start()

    step_rows = tok // 2

    def rows_of(y, h):
        return pl.ds((y * 2 + me.c) * tok + h * step_rows, step_rows)

    def fetch(h):
        at = rows_of(me.y, h)
        return remote(inputs.at[at], xo.at[at], s1.at[h], r1.at[h], me.step(dz=2))

    def across(h, d):
        at = rows_of(me.y, h)
        return remote(xo.at[at], xo.at[at], sy.at[h, d], ry.at[h, d], me.step(dy=dirs[d][1]))

    def onto(h, d):
        at = pl.ds((y_at(-dirs[d][1]) * 2 + me.c) * tok + h * step_rows + d * (step_rows // 2), step_rows // 2)
        return remote(xo.at[at], xo.at[at], sf.at[h, d], rf.at[h, d], me.step(dy=dirs[d][1]))

    def share(h, k):
        at = rows_of(y_at((0, -1, 1, 2)[k]), h)
        return remote(xo.at[at], xo.at[at], sc.at[h, k], rc.at[h, k], me.step(dc=1))

    for h in range(2):
        send_unit(3 * h)
        send_unit(3 * h + 1)
        fetch(h).start()
        send_unit(3 * h + 2)

    def spread(k):
        s = slot * (k % 2) + (1 - slot) * (k // PIECES)
        p = slot * (k // 2) + (1 - slot) * (k % PIECES)
        here = wf.at[0, s, piece(p)]
        pltpu.make_async_copy(here, here, zr.at[s, p]).wait()

        @pl.when(me.inner & (s == 1))
        def _():
            remote(here, here, fs.at[p], zr.at[s, p], me.to_outer).start()

        for d, dx in dirs:
            remote(here, wf.at[1 + d, s, piece(p)], xs.at[d, s, p], xr.at[d, s, p], me.step(dx=dx)).start()

    def pass_on(p):
        for d, dx in dirs:
            there = wf.at[1 + d, d, piece(p)]
            remote(there, there, gs.at[d, p], xr.at[d, d, p], me.step(dx=dx)).wait_recv()
            remote(there, wf.at[3, d, piece(p)], gs.at[d, p], gr.at[d, p], me.step(dx=dx)).start()

    def straight(d, p):
        return remote(
            dw.at[2 - d, 1 - d, :, block(p)], near.at[d, 1 - d, :, block(p)],
            pns.at[d, 1 - d, p], pnr.at[d, 1 - d, p], me.step(dx=dirs[d][1]),
        )

    def opposite(d, p):
        return remote(
            dw.at[3, d, :, block(p)], far.at[d, :, block(p)], pfs.at[d, p], pfr.at[d, p], me.step(dx=dirs[d][1])
        )

    def onward(d, p):
        return remote(
            far.at[d, :, block(p)], near.at[d, d, :, block(p)], pns.at[d, d, p], pnr.at[d, d, p], me.step(dx=dirs[d][1])
        )

    def compute(xh, xl, stage, cstage):
        def split_inputs(source, s):
            n = 128
            loads = [
                pltpu.make_async_copy(source.at[pl.ds(i * n, n)], stage.at[i % 2, pl.ds(0, n)], ls.at[i % 2])
                for i in range(tokens // n)
            ]
            loads[0].start()
            for i in range(tokens // n):
                if i + 1 < len(loads):
                    loads[i + 1].start()
                loads[i].wait()

                def strip(at):
                    high, low = split(stage[i % 2, pl.ds(at, 16)])
                    to = pl.ds(pl.multiple_of(i * n + at, 16), 16)
                    xh[to, s * half : (s + 1) * half] = high
                    xl[to, s * half : (s + 1) * half] = low

                strips(n // 16, 16, strip)

        def split_weight(units):
            loads = [
                pltpu.make_async_copy(wf.at[j, s], stage.at[i % 2], ls.at[i % 2]) for i, (j, s) in enumerate(units)
            ]
            loads[0].start()
            for i, (j, s) in enumerate(units):
                if i + 1 < len(loads):
                    loads[i + 1].start()
                loads[i].wait()

                def strip(at):
                    high, low = split(stage[i % 2, pl.ds(at, 16)])
                    to = pl.ds(pl.multiple_of(j * r + at, 16), 16)
                    wh[to, s * half : (s + 1) * half] = high
                    wl[to, s * half : (s + 1) * half] = low

                strips(r // 16, 16, strip)

        def turn_cotangent(j):
            column = me.x_plus[(0, 3, 1, 2)[j]] * (2 * r)
            n = cstage.shape[1]
            loads = [
                pltpu.make_async_copy(
                    cot.at[pl.ds(i * n, n), pl.ds(pl.multiple_of(column, 128), 2 * r)], cstage.at[i % 2], ls.at[i % 2]
                )
                for i in range(tokens // n)
            ]
            loads[0].start()
            for i in range(len(loads)):
                if i + 1 < len(loads):
                    loads[i + 1].start()
                loads[i].wait()
                turned = cstage[i % 2].T
                dw[j, 1, :, i * n : (i + 1) * n] = jnp.where(me.zh == 0, turned[:r], turned[r:])

        def preact(j, count, s):
            of = slice(s * half, (s + 1) * half)

            def tile(at):
                to = pl.ds(at, 256)
                left = slice(j * r, (j + count) * r)
                value = (
                    dot(wh[left, of], xh[to, of], 1, 1)
                    + dot(wl[left, of], xh[to, of], 1, 1)
                    + dot(wh[left, of], xl[to, of], 1, 1)
                )
                for i in range(count):
                    new = value[i * r : (i + 1) * r]
                    dw[j + i, 0, :, to] = new if s == 0 else dw[j + i, 0, :, to] + new

            strips(tokens // 256, 256, tile)

        def pre_grad(j):
            def strip(at):
                from_ = pl.ds(at, 16)
                grad = dw[j, 1, from_, :tokens] * gelu_slope(dw[j, 0, from_, :tokens])
                to = pl.ds(pl.multiple_of(j * r + at, 16), 16)
                gh[to], gl[to] = split(grad)

            strips(r // 16, 16, strip)

        def weight_grad(j, count, s, first, tiles):
            left = slice(j * r, (j + count) * r)
            wide = 2 * cols

            def tile(at):
                to = pl.ds(pl.multiple_of(first * wide + at, wide), wide)
                of = pl.ds(pl.multiple_of(s * half + first * wide + at, wide), wide)
                value = (
                    dot(gh[left], xh[:, of], 1, 0) + dot(gl[left], xh[:, of], 1, 0) + dot(gh[left], xl[:, of], 1, 0)
                )
                for i in range(count):
                    dw[j + i, s, :, to] = value[i * r : (i + 1) * r]

            strips(tiles, wide, tile)

        def fetched(h):
            fetch(h).wait_recv()
            for d in range(2):
                across(h, d).start()
            share(h, 0).start()

        def crossed(h):
            for d in range(2):
                across(h, d).wait_recv()
                onto(h, d).start()
                share(h, 1 + d).start()

        def met(h):
            for d in range(2):
                onto(h, d).wait_recv()
            share(h, 3).start()

        for k in range(4):
            spread(k)
        split_inputs(inputs, 0)
        fetched(0)
        for k in range(4, 8):
            spread(k)
        turn_cotangent(0)
        turn_cotangent(1)
        crossed(0)
        fetched(1)
        turn_cotangent(2)
        met(0)
        for k in range(8, 12):
            spread(k)
        turn_cotangent(3)
        pass_on(0)
        split_weight([(0, 0), (0, 1)])
        crossed(1)
        preact(0, 1, 0)
        pass_on(1)
        met(1)
        pass_on(2)
        for h in range(2):
            for k in range(4):
                share(h, k).wait_recv()
        split_inputs(xo, 1)
        preact(0, 1, 1)
        pre_grad(0)
        pass_on(3)
        weight_grad(0, 1, 0, 0, 3)
        pass_on(4)
        weight_grad(0, 1, 1, 0, 3)
        pass_on(5)
        for d in range(2):
            for p in range(PIECES):
                unit = wf.at[1 + d, 1 - d, piece(p)]
                remote(unit, unit, xs.at[d, 1 - d, p], xr.at[d, 1 - d, p], me.step(dc=1)).wait_recv()
        split_weight([(1, 0), (1, 1), (2, 0), (2, 1)])
        preact(1, 2, 0)
        preact(1, 2, 1)
        pre_grad(1)
        pre_grad(2)
        for p in range(PIECES // 2):
            for d in (1, 0):
                weight_grad(1, 2, 1 - d, p, 1)
                if p < EARLY // 2:
                    straight(d, 2 * p).start()
                    straight(d, 2 * p + 1).start()
        for d in range(2):
            for p in range(PIECES):
                unit = wf.at[3, d, piece(p)]
                remote(unit, unit, gs.at[d, p], gr.at[d, p], me.step(dc=1)).wait_recv()
        split_weight([(3, 0), (3, 1)])
        preact(3, 1, 0)
        preact(3, 1, 1)
        pre_grad(3)
        for p in range(PIECES // 2):
            for d in range(2):
                weight_grad(3, 1, d, p, 1)
                if p < EARLY // 2:
                    opposite(d, 2 * p).start()
                    opposite(d, 2 * p + 1).start()

    f32, bf16 = jnp.float32, jnp.bfloat16
    pl.run_scoped(
        compute,
        pltpu.VMEM((tokens, 2 * half), bf16), pltpu.VMEM((tokens, 2 * half), bf16),
        pltpu.VMEM((2, r, half), f32), pltpu.VMEM((2, 256, 2 * r), f32),
    )

    def sums(acc):
        order = [(s, dy) for s in (1, 0) for dy in (2, 1, -1, 0)]
        shares = []
        y_copies = {}
        left = pl.ds(0, tokens // 2)
        right = pl.ds(tokens // 2, tokens // 2)
        side = (left, right)
        own = pl.ds(pl.multiple_of(me.c * r, r), r)
        others = pl.ds(pl.multiple_of((1 - me.c) * r, r), r)

        def input_grad(i):
            s, dy = order[i]
            of = pl.ds(pl.multiple_of(s * half + y_at(dy) * (2 * r), 128), 2 * r)
            acc[i] = dot(wh[:, of], gh[...], 0, 0) + dot(wl[:, of], gh[...], 0, 0) + dot(wh[:, of], gl[...], 0, 0)
            copy = remote(acc.at[i, others], cin.at[i], cs.at[i], cr.at[i], me.step(dc=1))
            copy.start()
            shares.append(copy)

        def on_chip(i):
            shares[i].wait_recv()
            acc[i, own] = acc[i, own] + cin[i]

        def y_start(i, d, kind, source, target, sems):
            copy = remote(source, target, sems[0], sems[1], me.step(dy=dirs[d][1]))
            copy.start()
            y_copies[i, d, kind] = copy

        def y_far(s):
            i = 4 * (1 - s)
            on_chip(i)
            for d in range(2):
                y_start(s, d, 0, acc.at[i, own, side[d]], yfar.at[s, d], (yfs.at[s, d], yfr.at[s, d]))

        def y_straight(s, d):
            i = 4 * (1 - s) + 1 + d
            on_chip(i)
            o = 1 - d
            y_start(s, d, 1, acc.at[i, own, side[o]], ynear.at[s, d, :, side[o]], (yns.at[s, d, o], ynr.at[s, d, o]))

        def y_pass(s):
            for d in range(2):
                i = 4 * (1 - s) + 1 + d
                y_copies[s, d, 0].wait_recv()
                yfar[s, d] = yfar[s, d] + acc[i, own, side[d]]
                y_start(s, d, 2, yfar.at[s, d], ynear.at[s, d, :, side[d]], (yns.at[s, d, d], ynr.at[s, d, d]))

        def y_sum(s):
            i = 4 * (1 - s) + 3
            for d in range(2):
                y_copies[s, d, 1].wait_recv()
                y_copies[s, d, 2].wait_recv()
            acc[i, own] = acc[i, own] + ynear[s, 0] + ynear[s, 1]

        def x_pass(p):
            for d, step in dirs:
                opposite(d, p).wait_recv()
                far[d, :, block(p)] = far[d, :, block(p)] + dw[2 - d, d, :, block(p)]
                onward(d, p).start()

        input_grad(0)
        input_grad(1)
        y_far(1)
        x_pass(0)
        x_pass(1)
        input_grad(2)
        y_straight(1, 0)
        input_grad(3)
        y_straight(1, 1)
        input_grad(4)
        x_pass(2)
        y_pass(1)
        on_chip(3)
        input_grad(5)
        y_far(0)
        x_pass(3)
        for p in range(EARLY, PIECES):
            for d in range(2):
                opposite(d, p).start()
        for p in range(EARLY, PIECES):
            for d in range(2):
                straight(d, p).start()
        input_grad(6)
        y_straight(0, 0)
        input_grad(7)
        y_straight(0, 1)
        on_chip(7)
        last = remote(acc.at[3, own], xz, s2, r2, me.step(dz=2))

        def x_sum(p):
            for d in range(2):
                straight(d, p).wait_recv()
                onward(d, p).wait_recv()
            for s in range(2):
                dw[0, s, :, block(p)] = dw[0, s, :, block(p)] + near[0, s, :, block(p)] + near[1, s, :, block(p)]

            @pl.when(me.outer)
            def _():
                remote(dw.at[0, 1, :, block(p)], zin.at[0, :, block(p)], qs.at[p], qr.at[0, p], me.to_inner).start()

            @pl.when(me.inner)
            def _():
                remote(dw.at[0, 0, :, block(p)], zin.at[1, :, block(p)], qs.at[p], qr.at[1, p], me.to_outer).start()

        def z_pass(p):
            @pl.when(me.inner)
            def _():
                here = zin.at[0, :, block(p)]
                remote(here, here, os_.at[p], qr.at[0, p], me.to_inner).wait_recv()
                zin[0, :, block(p)] = dw[0, 1, :, block(p)] + zin[0, :, block(p)]
                remote(here, zin.at[1, :, block(p)], os_.at[p], qr.at[1, p], me.to_inner).start()

        x_sum(0)
        x_sum(1)
        z_pass(0)
        x_sum(2)
        z_pass(1)
        x_sum(3)
        z_pass(2)
        y_sum(1)
        last.start()
        z_pass(3)
        x_pass(4)
        x_pass(5)
        y_pass(0)
        x_sum(4)
        z_pass(4)
        x_sum(5)
        z_pass(5)
        y_sum(0)
        last.wait_recv()
        acc[7, own] = acc[7, own] + xz[...]
        x_out = pltpu.make_async_copy(acc.at[7, own], xout, ls.at[0])
        x_out.start()
        for p in range(PIECES):
            here = zin.at[1, :, block(p)]
            remote(here, here, qs.at[p], qr.at[1, p], me.step(dz=1)).wait_recv()

            @pl.when(me.outer)
            def _():
                zin[1, :, block(p)] = dw[0, 0, :, block(p)] + zin[1, :, block(p)]

        w_out = pltpu.make_async_copy(zin.at[1], wout, ls.at[1])
        w_out.start()

        for p in range(PIECES):
            here = zin.at[1, :, block(p)]
            remote(here, here, qs.at[p], qr.at[1, p], me.step(dz=1)).wait_send()

            @pl.when(me.inner)
            def _():
                remote(here, here, os_.at[p], qr.at[0, p], me.step(dz=1)).wait_send()

        for p in range(PIECES):
            for d in range(2):
                for copy in (opposite(d, p), straight(d, p), onward(d, p)):
                    copy.wait_send()
            unit = wt.at[piece(p)]
            remote(unit, unit, zs.at[p], zs.at[p], me.step(dc=1)).wait_send()

            @pl.when(me.inner)
            def _():
                remote(unit, unit, fs.at[p], fs.at[p], me.step(dc=1)).wait_send()

            for d in range(2):
                for s in range(2):
                    remote(unit, unit, xs.at[d, s, p], xs.at[d, s, p], me.step(dc=1)).wait_send()
                remote(unit, unit, gs.at[d, p], gs.at[d, p], me.step(dc=1)).wait_send()
        for h in range(2):
            fetch(h).wait_send()
            for d in range(2):
                across(h, d).wait_send()
                onto(h, d).wait_send()
            for k in range(4):
                share(h, k).wait_send()
        for copy in list(y_copies.values()) + shares + [last]:
            copy.wait_send()
        x_out.wait()
        w_out.wait()

    pl.run_scoped(sums, pltpu.VMEM((8, 2 * r, tokens), f32))


def fused(inputs, wt, cot):
    dma = pltpu.SemaphoreType.DMA
    vmem = pltpu.VMEM
    f32, bf16 = jnp.float32, jnp.bfloat16
    r, d = wt.shape
    t = inputs.shape[0]
    hbm = pl.BlockSpec(memory_space=pltpu.HBM)
    n = PIECES
    return pl.pallas_call(
        kernel,
        out_shape=(
            jax.ShapeDtypeStruct((r, d), f32),
            jax.ShapeDtypeStruct((r, t), f32),
            jax.ShapeDtypeStruct((t, d), f32),
            jax.ShapeDtypeStruct((4, 2, r, d), f32),
        ),
        in_specs=[hbm] * 3,
        out_specs=(hbm,) * 4,
        scratch_shapes=[
            vmem((4 * r, 2 * d), bf16), vmem((4 * r, 2 * d), bf16), vmem((4 * r, t), bf16), vmem((4 * r, t), bf16),
            vmem((4, 2, r, d), f32), vmem((2, r, d), f32), vmem((2, 2, r, d), f32), vmem((2, r, d), f32),
            vmem((8, r, t), f32), vmem((2, 2, r, t // 2), f32), vmem((2, 2, r, t), f32), vmem((r, t), f32),
            dma((n,)), dma((2, n)), dma((n,)), dma((2, 2, n)), dma((2, 2, n)), dma((2, n)), dma((2, n)),
            dma((2,)), dma((2,)), dma((2, 2)), dma((2, 2)), dma((2, 2)), dma((2, 2)), dma((2, 4)), dma((2, 4)), dma((2,)),
            dma((2, n)), dma((2, n)), dma((2, 2, n)), dma((2, 2, n)), dma((n,)), dma((2, n)), dma((n,)),
            dma((8,)), dma((8,)), dma((2, 2)), dma((2, 2)), dma((2, 2, 2)), dma((2, 2, 2)), dma, dma,
        ],
        compiler_params=pltpu.CompilerParams(collective_id=0, has_side_effects=True, vmem_limit_bytes=60 << 20),
    )(inputs, wt, cot)[:2]


def local(inputs, weight, cotangent):
    wout, xout = fused(inputs, weight.T, cotangent)
    return (xout.T, wout.T)


def solution(mesh):
    torus = Mesh(mesh.devices.reshape(4, 2, 2, 4, 2), AXES)
    in_specs = (P(("x", "zl"), "zh"), P("zh", ("y", "c", "x", "zl")), P(("x", "zl"), ("y", "c")))
    out_specs = (P(("x", "zl"), ("zh", "y", "c")), P("zh", ("y", "c", "x", "zl")))
    return jax.shard_map(local, mesh=torus, in_specs=in_specs, out_specs=out_specs, check_vma=False)
```

```python
import jax
import jax.numpy as jnp
from jax import lax
from jax.experimental import pallas as pl
from jax.experimental.pallas import tpu as pltpu
from jax.sharding import Mesh
from jax.sharding import PartitionSpec as P

AXES = ("x", "zl", "zh", "y", "c")
MESH = pl.DeviceIdType.MESH
PIECES = 6
UNITS = PIECES - 1
EARLY = 4

inv_sqrt_two = 0.7071067811865476
inv_sqrt_two_pi = 0.3989422804014327


class Place:
    def __init__(self):
        self.x, self.zl, self.zh, self.y, self.c = (lax.axis_index(a) for a in AXES)
        self.z = 2 * self.zh + self.zl
        self.inner = self.zl != self.zh
        self.outer = self.zl == self.zh
        self.to_inner = self.at_z(self.z + 1 - 2 * self.zh)
        self.to_outer = self.at_z(3 * self.zh)
        self.x_plus = [lax.rem(self.x + d, 4) for d in range(4)]
        self.y_plus = [lax.rem(self.y + d, 4) for d in range(4)]
        self.known = {}
        for key in ((1, 0, 0, 0), (-1, 0, 0, 0), (0, 1, 0, 0), (0, -1, 0, 0), (0, 0, 1, 0), (0, 0, -1, 0), (0, 0, 2, 0), (0, 0, 0, 1)):
            self.known[key] = self.place(*key)

    def at_z(self, z):
        return (self.x, lax.rem(z, 2), lax.div(z, 2), self.y, self.c)

    def step(self, dx=0, dy=0, dz=0, dc=0):
        return self.known[dx, dy, dz, dc]

    def place(self, dx, dy, dz, dc):
        z = lax.rem(self.z + dz + 4, 4)
        return (
            lax.rem(self.x + dx + 4, 4),
            lax.rem(z, 2),
            lax.div(z, 2),
            lax.rem(self.y + dy + 4, 4),
            lax.rem(self.c + dc, 2),
        )


def enter(me):
    barrier = pltpu.get_barrier_semaphore()
    steps = [
        dict(dx=1), dict(dx=-1), dict(dy=1), dict(dy=-1),
        dict(dz=1), dict(dz=-1), dict(dz=2), dict(dc=1),
    ]
    for step in steps:
        pl.semaphore_signal(barrier, inc=1, device_id=me.step(**step), device_id_type=MESH)
    pl.semaphore_wait(barrier, len(steps))


def remote(src, dst, send, recv, device):
    return pltpu.make_async_remote_copy(
        src_ref=src, dst_ref=dst, send_sem=send, recv_sem=recv, device_id=device, device_id_type=MESH
    )


def dot(left, right, left_dim, right_dim):
    return lax.dot_general(
        left, right, (((left_dim,), (right_dim,)), ((), ())), preferred_element_type=jnp.float32
    )


def gelu_slope(preact):
    cumulative = 0.5 * (1.0 + lax.erf(preact * inv_sqrt_two))
    density = jnp.exp(-0.5 * preact * preact) * inv_sqrt_two_pi
    return cumulative + preact * density


def split(value):
    high = value.astype(jnp.bfloat16)
    return high, (value - high.astype(jnp.float32)).astype(jnp.bfloat16)


def strips(count, size, body):
    def one(i, carry):
        body(pl.multiple_of(i * size, size))
        return carry

    lax.fori_loop(0, count, one, 0)


def kernel(
    inputs, wt, cot, wout, xout, xo, wf, wrow,
    wh, wl, gh, gl, dw, far, near, zin, cin, yfar, ynear, xz,
    zs, zr, fs, xs, xr, gs, gr, s1, r1, sy, ry, sf, rf, sc, rc, ls,
    pfs, pfr, pns, pnr, qs, qr, os_, cs, cr, yfs, yfr, yns, ynr, s2, r2,
    bxs, bxr, bgs, bgr, bzs, bzr, bfs,
):
    me = Place()
    r, half = wt.shape
    tokens = inputs.shape[0]
    rows = r // PIECES
    cols = half // PIECES
    tok = tokens // 8
    dirs = ((0, 1), (1, -1))

    def piece(p):
        return pl.ds(p * rows, rows)

    def block(p):
        return pl.ds(p * cols, cols)

    def y_at(d):
        return me.y_plus[d % 4]

    enter(me)

    slot = me.zl + me.zh - 2 * me.zl * me.zh
    def send_unit(p):
        remote(wt.at[piece(p)], wf.at[0, slot, piece(p)], zs.at[p], zr.at[slot, p], me.to_inner).start()

        @pl.when(me.outer)
        def _():
            pltpu.make_async_copy(wt.at[piece(p)], wf.at[0, 0, piece(p)], zr.at[0, p]).start()

    step_rows = tok // 2

    def rows_of(y, h):
        return pl.ds((y * 2 + me.c) * tok + h * step_rows, step_rows)

    def fetch(h):
        at = rows_of(me.y, h)
        return remote(inputs.at[at], xo.at[at], s1.at[h], r1.at[h], me.step(dz=2))

    def across(h, d):
        at = rows_of(me.y, h)
        return remote(xo.at[at], xo.at[at], sy.at[h, d], ry.at[h, d], me.step(dy=dirs[d][1]))

    def onto(h, d):
        at = pl.ds((y_at(-dirs[d][1]) * 2 + me.c) * tok + h * step_rows + d * (step_rows // 2), step_rows // 2)
        return remote(xo.at[at], xo.at[at], sf.at[h, d], rf.at[h, d], me.step(dy=dirs[d][1]))

    def share(h, k):
        at = rows_of(y_at((0, -1, 1, 2)[k]), h)
        return remote(xo.at[at], xo.at[at], sc.at[h, k], rc.at[h, k], me.step(dc=1))

    turned = piece(UNITS)

    def row_out(d):
        return remote(wt.at[turned], wrow.at[1 + d], bxs.at[d], bxr.at[d], me.step(dx=dirs[d][1]))

    def row_on(d):
        at = pl.ds(d * (rows // 2), rows // 2)
        return remote(wrow.at[1 + d, at], wrow.at[3, at], bgs.at[d], bgr.at[d], me.step(dx=dirs[d][1]))

    def row_z(j):
        source = wt.at[turned] if j == 0 else wrow.at[j]
        remote(source, wf.at[j, slot, turned], bzs.at[j], bzr.at[j, slot], me.to_inner).start()

        @pl.when(me.outer)
        def _():
            pltpu.make_async_copy(source, wf.at[j, 0, turned], bzr.at[j, 0]).start()

    def row_pass(j):
        for s in range(2):
            here = wf.at[j, s, turned]
            pltpu.make_async_copy(here, here, bzr.at[j, s]).wait()

        @pl.when(me.inner)
        def _():
            here = wf.at[j, 1, turned]
            remote(here, here, bfs.at[j], bzr.at[j, 1], me.to_outer).start()

    for d in range(2):
        row_out(d).start()
    send_unit(0)
    send_unit(1)
    fetch(0).start()
    for p in range(2, UNITS):
        send_unit(p)
    fetch(1).start()
    row_z(0)

    def spread(k):
        s = slot * (k % 2) + (1 - slot) * (k // UNITS)
        p = slot * (k // 2) + (1 - slot) * (k % UNITS)
        here = wf.at[0, s, piece(p)]
        pltpu.make_async_copy(here, here, zr.at[s, p]).wait()

        @pl.when(me.inner & (s == 1))
        def _():
            remote(here, here, fs.at[p], zr.at[s, p], me.to_outer).start()

        for d, dx in dirs:
            remote(here, wf.at[1 + d, s, piece(p)], xs.at[d, s, p], xr.at[d, s, p], me.step(dx=dx)).start()

    def pass_on(p):
        for d, dx in dirs:
            there = wf.at[1 + d, d, piece(p)]
            remote(there, there, gs.at[d, p], xr.at[d, d, p], me.step(dx=dx)).wait_recv()
            remote(there, wf.at[3, d, piece(p)], gs.at[d, p], gr.at[d, p], me.step(dx=dx)).start()

    def straight(d, p):
        return remote(
            dw.at[2 - d, 1 - d, :, block(p)], near.at[d, 1 - d, :, block(p)],
            pns.at[d, 1 - d, p], pnr.at[d, 1 - d, p], me.step(dx=dirs[d][1]),
        )

    def opposite(d, p):
        return remote(
            dw.at[3, d, :, block(p)], far.at[d, :, block(p)], pfs.at[d, p], pfr.at[d, p], me.step(dx=dirs[d][1])
        )

    def onward(d, p):
        return remote(
            far.at[d, :, block(p)], near.at[d, d, :, block(p)], pns.at[d, d, p], pnr.at[d, d, p], me.step(dx=dirs[d][1])
        )

    def compute(xh, xl, stage, cstage):
        def split_inputs(source, s):
            n = 128
            loads = [
                pltpu.make_async_copy(source.at[pl.ds(i * n, n)], stage.at[i % 2, pl.ds(0, n)], ls.at[i % 2])
                for i in range(tokens // n)
            ]
            loads[0].start()
            for i in range(tokens // n):
                if i + 1 < len(loads):
                    loads[i + 1].start()
                loads[i].wait()

                def strip(at):
                    high, low = split(stage[i % 2, pl.ds(at, 16)])
                    to = pl.ds(pl.multiple_of(i * n + at, 16), 16)
                    xh[to, s * half : (s + 1) * half] = high
                    xl[to, s * half : (s + 1) * half] = low

                strips(n // 16, 16, strip)

        def split_weight(units):
            loads = [
                pltpu.make_async_copy(wf.at[j, s], stage.at[i % 2], ls.at[i % 2]) for i, (j, s) in enumerate(units)
            ]
            loads[0].start()
            for i, (j, s) in enumerate(units):
                if i + 1 < len(loads):
                    loads[i + 1].start()
                loads[i].wait()

                def strip(at):
                    high, low = split(stage[i % 2, pl.ds(at, 16)])
                    to = pl.ds(pl.multiple_of(j * r + at, 16), 16)
                    wh[to, s * half : (s + 1) * half] = high
                    wl[to, s * half : (s + 1) * half] = low

                strips(r // 16, 16, strip)

        def turn_cotangent(j):
            column = me.x_plus[(0, 3, 1, 2)[j]] * (2 * r)
            n = cstage.shape[1]
            loads = [
                pltpu.make_async_copy(
                    cot.at[pl.ds(i * n, n), pl.ds(pl.multiple_of(column, 128), 2 * r)], cstage.at[i % 2], ls.at[i % 2]
                )
                for i in range(tokens // n)
            ]
            loads[0].start()
            for i in range(len(loads)):
                if i + 1 < len(loads):
                    loads[i + 1].start()
                loads[i].wait()
                turned = cstage[i % 2].T
                dw[j, 1, :, i * n : (i + 1) * n] = jnp.where(me.zh == 0, turned[:r], turned[r:])

        def preact(j, count, s):
            of = slice(s * half, (s + 1) * half)

            def tile(at):
                to = pl.ds(at, 256)
                left = slice(j * r, (j + count) * r)
                value = (
                    dot(wh[left, of], xh[to, of], 1, 1)
                    + dot(wl[left, of], xh[to, of], 1, 1)
                    + dot(wh[left, of], xl[to, of], 1, 1)
                )
                for i in range(count):
                    new = value[i * r : (i + 1) * r]
                    dw[j + i, 0, :, to] = new if s == 0 else dw[j + i, 0, :, to] + new

            strips(tokens // 256, 256, tile)

        def pre_grad(j):
            def strip(at):
                from_ = pl.ds(at, 16)
                grad = dw[j, 1, from_, :tokens] * gelu_slope(dw[j, 0, from_, :tokens])
                to = pl.ds(pl.multiple_of(j * r + at, 16), 16)
                gh[to], gl[to] = split(grad)

            strips(r // 16, 16, strip)

        def weight_grad(j, count, s, first, tiles):
            left = slice(j * r, (j + count) * r)
            wide = 2 * cols

            def tile(at):
                to = pl.ds(pl.multiple_of(first * wide + at, wide), wide)
                of = pl.ds(pl.multiple_of(s * half + first * wide + at, wide), wide)
                value = (
                    dot(gh[left], xh[:, of], 1, 0) + dot(gl[left], xh[:, of], 1, 0) + dot(gh[left], xl[:, of], 1, 0)
                )
                for i in range(count):
                    dw[j + i, s, :, to] = value[i * r : (i + 1) * r]

            strips(tiles, wide, tile)

        def fetched(h):
            fetch(h).wait_recv()
            for d in range(2):
                across(h, d).start()
            share(h, 0).start()

        def crossed(h):
            for d in range(2):
                across(h, d).wait_recv()
                onto(h, d).start()
                share(h, 1 + d).start()

        def met(h):
            for d in range(2):
                onto(h, d).wait_recv()
            share(h, 3).start()

        for k in range(4):
            spread(k)
        for d in range(2):
            row_out(d).wait_recv()
            row_on(d).start()
            row_z(1 + d)
        split_inputs(inputs, 0)
        fetched(0)
        for k in range(4, 7):
            spread(k)
        turn_cotangent(0)
        turn_cotangent(1)
        crossed(0)
        fetched(1)
        for d in range(2):
            row_on(d).wait_recv()
        row_z(3)
        turn_cotangent(2)
        met(0)
        for k in range(7, 2 * UNITS):
            spread(k)
        turn_cotangent(3)
        pass_on(0)
        row_pass(0)
        split_weight([(0, 0), (0, 1)])
        crossed(1)
        preact(0, 1, 0)
        pass_on(1)
        met(1)
        pass_on(2)
        row_pass(1)
        for h in range(2):
            for k in range(4):
                share(h, k).wait_recv()
        split_inputs(xo, 1)
        pass_on(3)
        row_pass(2)
        preact(0, 1, 1)
        pass_on(4)
        row_pass(3)
        pre_grad(0)
        for d in range(2):
            for p in range(UNITS):
                unit = wf.at[1 + d, 1 - d, piece(p)]
                remote(unit, unit, xs.at[d, 1 - d, p], xr.at[d, 1 - d, p], me.step(dc=1)).wait_recv()
        split_weight([(1, 0), (1, 1), (2, 0), (2, 1)])
        preact(1, 2, 0)
        preact(1, 2, 1)
        pre_grad(1)
        pre_grad(2)
        for p in range(EARLY // 2):
            for d in (1, 0):
                weight_grad(1, 2, 1 - d, p, 1)
                straight(d, 2 * p).start()
                straight(d, 2 * p + 1).start()
        for d in range(2):
            for p in range(UNITS):
                unit = wf.at[3, d, piece(p)]
                remote(unit, unit, gs.at[d, p], gr.at[d, p], me.step(dc=1)).wait_recv()
        split_weight([(3, 0), (3, 1)])
        preact(3, 1, 0)
        preact(3, 1, 1)
        pre_grad(3)
        for p in range(EARLY // 2):
            for d in range(2):
                weight_grad(3, 1, d, p, 1)
                opposite(d, 2 * p).start()
                opposite(d, 2 * p + 1).start()
        for s in range(2):
            weight_grad(0, 3, s, EARLY // 2, PIECES // 2 - EARLY // 2)
            weight_grad(3, 1, s, EARLY // 2, PIECES // 2 - EARLY // 2)
            weight_grad(0, 1, s, 0, EARLY // 2)

    f32, bf16 = jnp.float32, jnp.bfloat16
    pl.run_scoped(
        compute,
        pltpu.VMEM((tokens, 2 * half), bf16), pltpu.VMEM((tokens, 2 * half), bf16),
        pltpu.VMEM((2, r, half), f32), pltpu.VMEM((2, 256, 2 * r), f32),
    )

    def sums(acc):
        order = [(s, dy) for s in (1, 0) for dy in (2, 1, -1, 0)]
        shares = []
        y_copies = {}
        left = pl.ds(0, tokens // 2)
        right = pl.ds(tokens // 2, tokens // 2)
        side = (left, right)
        own = pl.ds(pl.multiple_of(me.c * r, r), r)
        others = pl.ds(pl.multiple_of((1 - me.c) * r, r), r)

        def input_grad(i):
            s, dy = order[i]
            of = pl.ds(pl.multiple_of(s * half + y_at(dy) * (2 * r), 128), 2 * r)
            acc[i] = dot(wh[:, of], gh[...], 0, 0) + dot(wl[:, of], gh[...], 0, 0) + dot(wh[:, of], gl[...], 0, 0)
            copy = remote(acc.at[i, others], cin.at[i], cs.at[i], cr.at[i], me.step(dc=1))
            copy.start()
            shares.append(copy)

        def on_chip(i):
            shares[i].wait_recv()
            acc[i, own] = acc[i, own] + cin[i]

        def y_start(i, d, kind, source, target, sems):
            copy = remote(source, target, sems[0], sems[1], me.step(dy=dirs[d][1]))
            copy.start()
            y_copies[i, d, kind] = copy

        def y_far(s):
            i = 4 * (1 - s)
            on_chip(i)
            for d in range(2):
                y_start(s, d, 0, acc.at[i, own, side[d]], yfar.at[s, d], (yfs.at[s, d], yfr.at[s, d]))

        def y_straight(s, d):
            i = 4 * (1 - s) + 1 + d
            on_chip(i)
            o = 1 - d
            y_start(s, d, 1, acc.at[i, own, side[o]], ynear.at[s, d, :, side[o]], (yns.at[s, d, o], ynr.at[s, d, o]))

        def y_pass(s):
            for d in range(2):
                i = 4 * (1 - s) + 1 + d
                y_copies[s, d, 0].wait_recv()
                yfar[s, d] = yfar[s, d] + acc[i, own, side[d]]
                y_start(s, d, 2, yfar.at[s, d], ynear.at[s, d, :, side[d]], (yns.at[s, d, d], ynr.at[s, d, d]))

        def y_sum(s):
            i = 4 * (1 - s) + 3
            for d in range(2):
                y_copies[s, d, 1].wait_recv()
                y_copies[s, d, 2].wait_recv()
            acc[i, own] = acc[i, own] + ynear[s, 0] + ynear[s, 1]

        def x_pass(p):
            for d, step in dirs:
                opposite(d, p).wait_recv()
                far[d, :, block(p)] = far[d, :, block(p)] + dw[2 - d, d, :, block(p)]
                onward(d, p).start()

        def x_sum(p):
            for d in range(2):
                straight(d, p).wait_recv()
                onward(d, p).wait_recv()
            for s in range(2):
                dw[0, s, :, block(p)] = dw[0, s, :, block(p)] + near[0, s, :, block(p)] + near[1, s, :, block(p)]

            @pl.when(me.outer)
            def _():
                remote(dw.at[0, 1, :, block(p)], zin.at[0, :, block(p)], qs.at[p], qr.at[0, p], me.to_inner).start()

            @pl.when(me.inner)
            def _():
                remote(dw.at[0, 0, :, block(p)], zin.at[1, :, block(p)], qs.at[p], qr.at[1, p], me.to_outer).start()

        def z_pass(p):
            @pl.when(me.inner)
            def _():
                here = zin.at[0, :, block(p)]
                remote(here, here, os_.at[p], qr.at[0, p], me.to_inner).wait_recv()
                zin[0, :, block(p)] = dw[0, 1, :, block(p)] + zin[0, :, block(p)]
                remote(here, zin.at[1, :, block(p)], os_.at[p], qr.at[1, p], me.to_inner).start()

        input_grad(0)
        input_grad(1)
        y_far(1)
        for p in range(EARLY):
            x_pass(p)
        for p in range(EARLY, PIECES):
            for d in range(2):
                opposite(d, p).start()
        for p in range(EARLY, PIECES):
            for d in range(2):
                straight(d, p).start()
        input_grad(2)
        y_straight(1, 0)
        x_sum(0)
        input_grad(3)
        y_straight(1, 1)
        x_sum(1)
        z_pass(0)
        input_grad(4)
        y_pass(1)
        x_sum(2)
        z_pass(1)
        on_chip(3)
        input_grad(5)
        y_far(0)
        x_sum(3)
        z_pass(2)
        input_grad(6)
        y_straight(0, 0)
        input_grad(7)
        y_straight(0, 1)
        on_chip(7)
        z_pass(3)
        x_pass(4)
        x_pass(5)
        y_sum(1)
        last = remote(acc.at[3, own], xz, s2, r2, me.step(dz=2))
        last.start()
        y_pass(0)
        x_sum(4)
        z_pass(4)
        x_sum(5)
        z_pass(5)
        y_sum(0)
        last.wait_recv()
        acc[7, own] = acc[7, own] + xz[...]
        x_out = pltpu.make_async_copy(acc.at[7, own], xout, ls.at[0])
        x_out.start()
        for p in range(PIECES):
            here = zin.at[1, :, block(p)]
            remote(here, here, qs.at[p], qr.at[1, p], me.step(dz=1)).wait_recv()

            @pl.when(me.outer)
            def _():
                zin[1, :, block(p)] = dw[0, 0, :, block(p)] + zin[1, :, block(p)]

        w_out = pltpu.make_async_copy(zin.at[1], wout, ls.at[1])
        w_out.start()

        for p in range(PIECES):
            here = zin.at[1, :, block(p)]
            remote(here, here, qs.at[p], qr.at[1, p], me.step(dz=1)).wait_send()

            @pl.when(me.inner)
            def _():
                remote(here, here, os_.at[p], qr.at[0, p], me.step(dz=1)).wait_send()

        for p in range(PIECES):
            for d in range(2):
                for copy in (opposite(d, p), straight(d, p), onward(d, p)):
                    copy.wait_send()
        for p in range(UNITS):
            unit = wt.at[piece(p)]
            remote(unit, unit, zs.at[p], zs.at[p], me.step(dc=1)).wait_send()

            @pl.when(me.inner)
            def _():
                remote(unit, unit, fs.at[p], fs.at[p], me.step(dc=1)).wait_send()

            for d in range(2):
                for s in range(2):
                    remote(unit, unit, xs.at[d, s, p], xs.at[d, s, p], me.step(dc=1)).wait_send()
                remote(unit, unit, gs.at[d, p], gs.at[d, p], me.step(dc=1)).wait_send()
        for j in range(4):
            unit = wt.at[turned]
            remote(unit, unit, bzs.at[j], bzs.at[j], me.step(dc=1)).wait_send()

            @pl.when(me.inner)
            def _():
                remote(unit, unit, bfs.at[j], bfs.at[j], me.step(dc=1)).wait_send()

        for d in range(2):
            row_out(d).wait_send()
            row_on(d).wait_send()
        for h in range(2):
            fetch(h).wait_send()
            for d in range(2):
                across(h, d).wait_send()
                onto(h, d).wait_send()
            for k in range(4):
                share(h, k).wait_send()
        for copy in list(y_copies.values()) + shares + [last]:
            copy.wait_send()
        x_out.wait()
        w_out.wait()

    pl.run_scoped(sums, pltpu.VMEM((8, 2 * r, tokens), f32))


def fused(inputs, wt, cot):
    dma = pltpu.SemaphoreType.DMA
    vmem = pltpu.VMEM
    f32, bf16 = jnp.float32, jnp.bfloat16
    r, d = wt.shape
    t = inputs.shape[0]
    hbm = pl.BlockSpec(memory_space=pltpu.HBM)
    n, u = PIECES, UNITS
    return pl.pallas_call(
        kernel,
        out_shape=(
            jax.ShapeDtypeStruct((r, d), f32),
            jax.ShapeDtypeStruct((r, t), f32),
            jax.ShapeDtypeStruct((t, d), f32),
            jax.ShapeDtypeStruct((4, 2, r, d), f32),
            jax.ShapeDtypeStruct((4, r // n, d), f32),
        ),
        in_specs=[hbm] * 3,
        out_specs=(hbm,) * 5,
        scratch_shapes=[
            vmem((4 * r, 2 * d), bf16), vmem((4 * r, 2 * d), bf16), vmem((4 * r, t), bf16), vmem((4 * r, t), bf16),
            vmem((4, 2, r, d), f32), vmem((2, r, d), f32), vmem((2, 2, r, d), f32), vmem((2, r, d), f32),
            vmem((8, r, t), f32), vmem((2, 2, r, t // 2), f32), vmem((2, 2, r, t), f32), vmem((r, t), f32),
            dma((u,)), dma((2, u)), dma((u,)), dma((2, 2, u)), dma((2, 2, u)), dma((2, u)), dma((2, u)),
            dma((2,)), dma((2,)), dma((2, 2)), dma((2, 2)), dma((2, 2)), dma((2, 2)), dma((2, 4)), dma((2, 4)), dma((2,)),
            dma((2, n)), dma((2, n)), dma((2, 2, n)), dma((2, 2, n)), dma((n,)), dma((2, n)), dma((n,)),
            dma((8,)), dma((8,)), dma((2, 2)), dma((2, 2)), dma((2, 2, 2)), dma((2, 2, 2)), dma, dma,
            dma((2,)), dma((2,)), dma((2,)), dma((2,)), dma((4,)), dma((4, 2)), dma((4,)),
        ],
        compiler_params=pltpu.CompilerParams(collective_id=0, has_side_effects=True, vmem_limit_bytes=60 << 20),
    )(inputs, wt, cot)[:2]


def local(inputs, weight, cotangent):
    wout, xout = fused(inputs, weight.T, cotangent)
    return (xout.T, wout.T)


def solution(mesh):
    torus = Mesh(mesh.devices.reshape(4, 2, 2, 4, 2), AXES)
    in_specs = (P(("x", "zl"), "zh"), P("zh", ("y", "c", "x", "zl")), P(("x", "zl"), ("y", "c")))
    out_specs = (P(("x", "zl"), ("zh", "y", "c")), P("zh", ("y", "c", "x", "zl")))
    return jax.shard_map(local, mesh=torus, in_specs=in_specs, out_specs=out_specs, check_vma=False)
```

```python
import jax
import jax.numpy as jnp
from jax import lax
from jax.experimental import pallas as pl
from jax.experimental.pallas import tpu as pltpu
from jax.sharding import Mesh
from jax.sharding import PartitionSpec as P

AXES = ("x", "zl", "zh", "y", "c")
MESH = pl.DeviceIdType.MESH
PIECES = 6
UNITS = PIECES - 1
EARLY = 4

inv_sqrt_two = 0.7071067811865476
inv_sqrt_two_pi = 0.3989422804014327


class Place:
    def __init__(self):
        self.x, self.zl, self.zh, self.y, self.c = (lax.axis_index(a) for a in AXES)
        self.z = 2 * self.zh + self.zl
        self.inner = self.zl != self.zh
        self.outer = self.zl == self.zh
        self.to_inner = self.at_z(self.z + 1 - 2 * self.zh)
        self.to_outer = self.at_z(3 * self.zh)
        self.x_plus = [lax.rem(self.x + d, 4) for d in range(4)]
        self.y_plus = [lax.rem(self.y + d, 4) for d in range(4)]
        self.known = {}
        for key in ((1, 0, 0, 0), (-1, 0, 0, 0), (0, 1, 0, 0), (0, -1, 0, 0), (0, 0, 1, 0), (0, 0, -1, 0), (0, 0, 2, 0), (0, 0, 0, 1)):
            self.known[key] = self.place(*key)

    def at_z(self, z):
        return (self.x, lax.rem(z, 2), lax.div(z, 2), self.y, self.c)

    def step(self, dx=0, dy=0, dz=0, dc=0):
        return self.known[dx, dy, dz, dc]

    def place(self, dx, dy, dz, dc):
        z = lax.rem(self.z + dz + 4, 4)
        return (
            lax.rem(self.x + dx + 4, 4),
            lax.rem(z, 2),
            lax.div(z, 2),
            lax.rem(self.y + dy + 4, 4),
            lax.rem(self.c + dc, 2),
        )


def enter(me):
    barrier = pltpu.get_barrier_semaphore()
    steps = [
        dict(dx=1), dict(dx=-1), dict(dy=1), dict(dy=-1),
        dict(dz=1), dict(dz=-1), dict(dz=2), dict(dc=1),
    ]
    for step in steps:
        pl.semaphore_signal(barrier, inc=1, device_id=me.step(**step), device_id_type=MESH)
    pl.semaphore_wait(barrier, len(steps))


def remote(src, dst, send, recv, device):
    return pltpu.make_async_remote_copy(
        src_ref=src, dst_ref=dst, send_sem=send, recv_sem=recv, device_id=device, device_id_type=MESH
    )


def dot(left, right, left_dim, right_dim):
    return lax.dot_general(
        left, right, (((left_dim,), (right_dim,)), ((), ())), preferred_element_type=jnp.float32
    )


def gelu_slope(preact):
    cumulative = 0.5 * (1.0 + lax.erf(preact * inv_sqrt_two))
    density = jnp.exp(-0.5 * preact * preact) * inv_sqrt_two_pi
    return cumulative + preact * density


def split(value):
    high = value.astype(jnp.bfloat16)
    return high, (value - high.astype(jnp.float32)).astype(jnp.bfloat16)


def strips(count, size, body):
    def one(i, carry):
        body(pl.multiple_of(i * size, size))
        return carry

    lax.fori_loop(0, count, one, 0)


def kernel(
    inputs, wt, cot, wout, xout, xo, wf, wrow,
    wh, wl, gh, gl, dw, far, near, zin, cin, yfar, ynear, xz,
    zs, zr, fs, xs, xr, gs, gr, s1, r1, sy, ry, sf, rf, sc, rc, ls,
    pfs, pfr, pns, pnr, qs, qr, os_, cs, cr, yfs, yfr, yns, ynr, s2, r2,
    bxs, bxr, bgs, bgr, bzs, bzr, bfs,
):
    me = Place()
    r, half = wt.shape
    tokens = inputs.shape[0]
    rows = r // PIECES
    cols = half // PIECES
    tok = tokens // 8
    dirs = ((0, 1), (1, -1))

    def piece(p):
        return pl.ds(p * rows, rows)

    def block(p):
        return pl.ds(p * cols, cols)

    def y_at(d):
        return me.y_plus[d % 4]

    enter(me)

    slot = me.zl + me.zh - 2 * me.zl * me.zh
    def send_unit(p):
        remote(wt.at[piece(p)], wf.at[0, slot, piece(p)], zs.at[p], zr.at[slot, p], me.to_inner).start()

        @pl.when(me.outer)
        def _():
            pltpu.make_async_copy(wt.at[piece(p)], wf.at[0, 0, piece(p)], zr.at[0, p]).start()

    step_rows = tok // 2

    def rows_of(y, h):
        return pl.ds((y * 2 + me.c) * tok + h * step_rows, step_rows)

    def fetch(h):
        at = rows_of(me.y, h)
        return remote(inputs.at[at], xo.at[at], s1.at[h], r1.at[h], me.step(dz=2))

    def across(h, d):
        at = rows_of(me.y, h)
        return remote(xo.at[at], xo.at[at], sy.at[h, d], ry.at[h, d], me.step(dy=dirs[d][1]))

    def onto(h, d):
        at = pl.ds((y_at(-dirs[d][1]) * 2 + me.c) * tok + h * step_rows + d * (step_rows // 2), step_rows // 2)
        return remote(xo.at[at], xo.at[at], sf.at[h, d], rf.at[h, d], me.step(dy=dirs[d][1]))

    def share(h, k):
        at = rows_of(y_at((0, -1, 1, 2)[k]), h)
        return remote(xo.at[at], xo.at[at], sc.at[h, k], rc.at[h, k], me.step(dc=1))

    turned = piece(UNITS)

    def row_out(d):
        return remote(wt.at[turned], wrow.at[1 + d], bxs.at[d], bxr.at[d], me.step(dx=dirs[d][1]))

    def row_on(d):
        at = pl.ds(d * (rows // 2), rows // 2)
        return remote(wrow.at[1 + d, at], wrow.at[3, at], bgs.at[d], bgr.at[d], me.step(dx=dirs[d][1]))

    def row_z(j):
        source = wt.at[turned] if j == 0 else wrow.at[j]
        remote(source, wf.at[j, slot, turned], bzs.at[j], bzr.at[j, slot], me.to_inner).start()

        @pl.when(me.outer)
        def _():
            pltpu.make_async_copy(source, wf.at[j, 0, turned], bzr.at[j, 0]).start()

    def row_pass(j):
        for s in range(2):
            here = wf.at[j, s, turned]
            pltpu.make_async_copy(here, here, bzr.at[j, s]).wait()

        @pl.when(me.inner)
        def _():
            here = wf.at[j, 1, turned]
            remote(here, here, bfs.at[j], bzr.at[j, 1], me.to_outer).start()

    for d in range(2):
        row_out(d).start()
    send_unit(0)
    send_unit(1)
    fetch(0).start()
    for p in range(2, UNITS):
        send_unit(p)
    fetch(1).start()
    row_z(0)

    def spread(k):
        s = slot * (k % 2) + (1 - slot) * (k // UNITS)
        p = slot * (k // 2) + (1 - slot) * (k % UNITS)
        here = wf.at[0, s, piece(p)]
        pltpu.make_async_copy(here, here, zr.at[s, p]).wait()

        @pl.when(me.inner & (s == 1))
        def _():
            remote(here, here, fs.at[p], zr.at[s, p], me.to_outer).start()

        for d, dx in dirs:
            remote(here, wf.at[1 + d, s, piece(p)], xs.at[d, s, p], xr.at[d, s, p], me.step(dx=dx)).start()

    def pass_on(p):
        for d, dx in dirs:
            there = wf.at[1 + d, d, piece(p)]
            remote(there, there, gs.at[d, p], xr.at[d, d, p], me.step(dx=dx)).wait_recv()
            remote(there, wf.at[3, d, piece(p)], gs.at[d, p], gr.at[d, p], me.step(dx=dx)).start()

    def straight(d, p):
        return remote(
            dw.at[2 - d, 1 - d, :, block(p)], near.at[d, 1 - d, :, block(p)],
            pns.at[d, 1 - d, p], pnr.at[d, 1 - d, p], me.step(dx=dirs[d][1]),
        )

    def opposite(d, p):
        return remote(
            dw.at[3, d, :, block(p)], far.at[d, :, block(p)], pfs.at[d, p], pfr.at[d, p], me.step(dx=dirs[d][1])
        )

    def onward(d, p):
        return remote(
            far.at[d, :, block(p)], near.at[d, d, :, block(p)], pns.at[d, d, p], pnr.at[d, d, p], me.step(dx=dirs[d][1])
        )

    def compute(xh, xl, stage, cstage):
        def split_inputs(source, s):
            n = 128
            loads = [
                pltpu.make_async_copy(source.at[pl.ds(i * n, n)], stage.at[i % 2, pl.ds(0, n)], ls.at[i % 2])
                for i in range(tokens // n)
            ]
            loads[0].start()
            for i in range(tokens // n):
                if i + 1 < len(loads):
                    loads[i + 1].start()
                loads[i].wait()

                def strip(at):
                    high, low = split(stage[i % 2, pl.ds(at, 16)])
                    to = pl.ds(pl.multiple_of(i * n + at, 16), 16)
                    xh[to, s * half : (s + 1) * half] = high
                    xl[to, s * half : (s + 1) * half] = low

                strips(n // 16, 16, strip)

        def split_weight(units):
            loads = [
                pltpu.make_async_copy(wf.at[j, s], stage.at[i % 2], ls.at[i % 2]) for i, (j, s) in enumerate(units)
            ]
            loads[0].start()
            for i, (j, s) in enumerate(units):
                if i + 1 < len(loads):
                    loads[i + 1].start()
                loads[i].wait()

                def strip(at):
                    high, low = split(stage[i % 2, pl.ds(at, 16)])
                    to = pl.ds(pl.multiple_of(j * r + at, 16), 16)
                    wh[to, s * half : (s + 1) * half] = high
                    wl[to, s * half : (s + 1) * half] = low

                strips(r // 16, 16, strip)

        def turn_cotangent(j):
            column = me.x_plus[(0, 3, 1, 2)[j]] * (2 * r)
            n = cstage.shape[1]
            loads = [
                pltpu.make_async_copy(
                    cot.at[pl.ds(i * n, n), pl.ds(pl.multiple_of(column, 128), 2 * r)], cstage.at[i % 2], ls.at[i % 2]
                )
                for i in range(tokens // n)
            ]
            loads[0].start()
            for i in range(len(loads)):
                if i + 1 < len(loads):
                    loads[i + 1].start()
                loads[i].wait()
                turned = cstage[i % 2].T
                dw[j, 1, :, i * n : (i + 1) * n] = jnp.where(me.zh == 0, turned[:r], turned[r:])

        def preact(j, count, s):
            of = slice(s * half, (s + 1) * half)

            def tile(at):
                to = pl.ds(at, 256)
                left = slice(j * r, (j + count) * r)
                value = (
                    dot(wh[left, of], xh[to, of], 1, 1)
                    + dot(wl[left, of], xh[to, of], 1, 1)
                    + dot(wh[left, of], xl[to, of], 1, 1)
                )
                for i in range(count):
                    new = value[i * r : (i + 1) * r]
                    dw[j + i, 0, :, to] = new if s == 0 else dw[j + i, 0, :, to] + new

            strips(tokens // 256, 256, tile)

        def pre_grad(j):
            def strip(at):
                from_ = pl.ds(at, 16)
                grad = dw[j, 1, from_, :tokens] * gelu_slope(dw[j, 0, from_, :tokens])
                to = pl.ds(pl.multiple_of(j * r + at, 16), 16)
                gh[to], gl[to] = split(grad)

            strips(r // 16, 16, strip)

        def weight_grad(j, count, s, first, tiles):
            left = slice(j * r, (j + count) * r)
            wide = 2 * cols

            def tile(at):
                to = pl.ds(pl.multiple_of(first * wide + at, wide), wide)
                of = pl.ds(pl.multiple_of(s * half + first * wide + at, wide), wide)
                value = (
                    dot(gh[left], xh[:, of], 1, 0) + dot(gl[left], xh[:, of], 1, 0) + dot(gh[left], xl[:, of], 1, 0)
                )
                for i in range(count):
                    dw[j + i, s, :, to] = value[i * r : (i + 1) * r]

            strips(tiles, wide, tile)

        def fetched(h):
            fetch(h).wait_recv()
            for d in range(2):
                across(h, d).start()
            share(h, 0).start()

        def crossed(h):
            for d in range(2):
                across(h, d).wait_recv()
                onto(h, d).start()
                share(h, 1 + d).start()

        def met(h):
            for d in range(2):
                onto(h, d).wait_recv()
            share(h, 3).start()

        for k in range(4):
            spread(k)
        for d in range(2):
            row_out(d).wait_recv()
            row_on(d).start()
            row_z(1 + d)
        split_inputs(inputs, 0)
        fetched(0)
        for k in range(4, 7):
            spread(k)
        turn_cotangent(0)
        turn_cotangent(1)
        crossed(0)
        fetched(1)
        for d in range(2):
            row_on(d).wait_recv()
        row_z(3)
        turn_cotangent(2)
        met(0)
        for k in range(7, 2 * UNITS):
            spread(k)
        turn_cotangent(3)
        pass_on(0)
        row_pass(0)
        split_weight([(0, 0), (0, 1)])
        crossed(1)
        preact(0, 1, 0)
        pass_on(1)
        met(1)
        pass_on(2)
        row_pass(1)
        for h in range(2):
            for k in range(4):
                share(h, k).wait_recv()
        split_inputs(xo, 1)
        pass_on(3)
        row_pass(2)
        preact(0, 1, 1)
        pass_on(4)
        row_pass(3)
        pre_grad(0)
        for d in range(2):
            for p in range(UNITS):
                unit = wf.at[1 + d, 1 - d, piece(p)]
                remote(unit, unit, xs.at[d, 1 - d, p], xr.at[d, 1 - d, p], me.step(dc=1)).wait_recv()
        split_weight([(1, 0), (1, 1), (2, 0), (2, 1)])
        preact(1, 2, 0)
        preact(1, 2, 1)
        pre_grad(1)
        pre_grad(2)
        for p in range(EARLY // 2):
            for d in (1, 0):
                weight_grad(1, 2, 1 - d, p, 1)
                straight(d, 2 * p).start()
                straight(d, 2 * p + 1).start()
        for d in range(2):
            for p in range(UNITS):
                unit = wf.at[3, d, piece(p)]
                remote(unit, unit, gs.at[d, p], gr.at[d, p], me.step(dc=1)).wait_recv()
        split_weight([(3, 0), (3, 1)])
        preact(3, 1, 0)
        preact(3, 1, 1)
        pre_grad(3)
        for p in range(EARLY // 2):
            for d in range(2):
                weight_grad(3, 1, d, p, 1)
                opposite(d, 2 * p).start()
                opposite(d, 2 * p + 1).start()
        for s in range(2):
            weight_grad(0, 3, s, EARLY // 2, PIECES // 2 - EARLY // 2)
            weight_grad(3, 1, s, EARLY // 2, PIECES // 2 - EARLY // 2)
            weight_grad(0, 1, s, 0, EARLY // 2)

    f32, bf16 = jnp.float32, jnp.bfloat16
    pl.run_scoped(
        compute,
        pltpu.VMEM((tokens, 2 * half), bf16), pltpu.VMEM((tokens, 2 * half), bf16),
        pltpu.VMEM((2, r, half), f32), pltpu.VMEM((2, 256, 2 * r), f32),
    )

    def sums(acc):
        order = [(s, dy) for s in (1, 0) for dy in (2, 1, -1, 0)]
        shares = []
        y_copies = {}
        left = pl.ds(0, tokens // 2)
        right = pl.ds(tokens // 2, tokens // 2)
        side = (left, right)
        own = pl.ds(pl.multiple_of(me.c * r, r), r)
        others = pl.ds(pl.multiple_of((1 - me.c) * r, r), r)

        def input_grad(i):
            s, dy = order[i]
            of = pl.ds(pl.multiple_of(s * half + y_at(dy) * (2 * r), 128), 2 * r)
            acc[i] = dot(wh[:, of], gh[...], 0, 0) + dot(wl[:, of], gh[...], 0, 0) + dot(wh[:, of], gl[...], 0, 0)
            copy = remote(acc.at[i, others], cin.at[i], cs.at[i], cr.at[i], me.step(dc=1))
            copy.start()
            shares.append(copy)

        def on_chip(i):
            shares[i].wait_recv()
            acc[i, own] = acc[i, own] + cin[i]

        def y_start(i, d, kind, source, target, sems):
            copy = remote(source, target, sems[0], sems[1], me.step(dy=dirs[d][1]))
            copy.start()
            y_copies[i, d, kind] = copy

        def y_far(s):
            i = 4 * (1 - s)
            on_chip(i)
            for d in range(2):
                y_start(s, d, 0, acc.at[i, own, side[d]], yfar.at[s, d], (yfs.at[s, d], yfr.at[s, d]))

        def y_straight(s, d):
            i = 4 * (1 - s) + 1 + d
            on_chip(i)
            o = 1 - d
            y_start(s, d, 1, acc.at[i, own, side[o]], ynear.at[s, d, :, side[o]], (yns.at[s, d, o], ynr.at[s, d, o]))

        def y_pass(s):
            for d in range(2):
                i = 4 * (1 - s) + 1 + d
                y_copies[s, d, 0].wait_recv()
                yfar[s, d] = yfar[s, d] + acc[i, own, side[d]]
                y_start(s, d, 2, yfar.at[s, d], ynear.at[s, d, :, side[d]], (yns.at[s, d, d], ynr.at[s, d, d]))

        def y_sum(s):
            i = 4 * (1 - s) + 3
            for d in range(2):
                y_copies[s, d, 1].wait_recv()
                y_copies[s, d, 2].wait_recv()
            acc[i, own] = acc[i, own] + ynear[s, 0] + ynear[s, 1]

        def x_pass(p):
            for d, step in dirs:
                opposite(d, p).wait_recv()
                far[d, :, block(p)] = far[d, :, block(p)] + dw[2 - d, d, :, block(p)]
                onward(d, p).start()

        def x_sum(p):
            for d in range(2):
                straight(d, p).wait_recv()
                onward(d, p).wait_recv()
            for s in range(2):
                dw[0, s, :, block(p)] = dw[0, s, :, block(p)] + near[0, s, :, block(p)] + near[1, s, :, block(p)]

            @pl.when(me.outer)
            def _():
                remote(dw.at[0, 1, :, block(p)], zin.at[0, :, block(p)], qs.at[p], qr.at[0, p], me.to_inner).start()

            @pl.when(me.inner)
            def _():
                remote(dw.at[0, 0, :, block(p)], zin.at[1, :, block(p)], qs.at[p], qr.at[1, p], me.to_outer).start()

        def z_pass(p):
            @pl.when(me.inner)
            def _():
                here = zin.at[0, :, block(p)]
                remote(here, here, os_.at[p], qr.at[0, p], me.to_inner).wait_recv()
                zin[0, :, block(p)] = dw[0, 1, :, block(p)] + zin[0, :, block(p)]
                remote(here, zin.at[1, :, block(p)], os_.at[p], qr.at[1, p], me.to_inner).start()

        input_grad(0)
        y_far(1)
        input_grad(1)
        for p in range(EARLY):
            x_pass(p)
        for p in range(EARLY, PIECES):
            for d in range(2):
                opposite(d, p).start()
        for p in range(EARLY, PIECES):
            for d in range(2):
                straight(d, p).start()
        input_grad(2)
        y_straight(1, 0)
        x_sum(0)
        input_grad(3)
        y_straight(1, 1)
        x_sum(1)
        z_pass(0)
        input_grad(4)
        y_pass(1)
        x_sum(2)
        z_pass(1)
        on_chip(3)
        input_grad(5)
        y_far(0)
        x_sum(3)
        z_pass(2)
        input_grad(6)
        y_straight(0, 0)
        input_grad(7)
        y_straight(0, 1)
        on_chip(7)
        z_pass(3)
        y_sum(1)
        last = remote(acc.at[3, own], xz, s2, r2, me.step(dz=2))
        last.start()
        x_pass(4)
        x_pass(5)
        y_pass(0)
        x_sum(4)
        z_pass(4)
        x_sum(5)
        z_pass(5)
        y_sum(0)
        last.wait_recv()
        acc[7, own] = acc[7, own] + xz[...]
        x_out = pltpu.make_async_copy(acc.at[7, own], xout, ls.at[0])
        x_out.start()
        for p in range(PIECES):
            here = zin.at[1, :, block(p)]
            remote(here, here, qs.at[p], qr.at[1, p], me.step(dz=1)).wait_recv()

            @pl.when(me.outer)
            def _():
                zin[1, :, block(p)] = dw[0, 0, :, block(p)] + zin[1, :, block(p)]

        w_out = pltpu.make_async_copy(zin.at[1], wout, ls.at[1])
        w_out.start()

        for p in range(PIECES):
            here = zin.at[1, :, block(p)]
            remote(here, here, qs.at[p], qr.at[1, p], me.step(dz=1)).wait_send()

            @pl.when(me.inner)
            def _():
                remote(here, here, os_.at[p], qr.at[0, p], me.step(dz=1)).wait_send()

        for p in range(PIECES):
            for d in range(2):
                for copy in (opposite(d, p), straight(d, p), onward(d, p)):
                    copy.wait_send()
        for p in range(UNITS):
            unit = wt.at[piece(p)]
            remote(unit, unit, zs.at[p], zs.at[p], me.step(dc=1)).wait_send()

            @pl.when(me.inner)
            def _():
                remote(unit, unit, fs.at[p], fs.at[p], me.step(dc=1)).wait_send()

            for d in range(2):
                for s in range(2):
                    remote(unit, unit, xs.at[d, s, p], xs.at[d, s, p], me.step(dc=1)).wait_send()
                remote(unit, unit, gs.at[d, p], gs.at[d, p], me.step(dc=1)).wait_send()
        for j in range(4):
            unit = wt.at[turned]
            remote(unit, unit, bzs.at[j], bzs.at[j], me.step(dc=1)).wait_send()

            @pl.when(me.inner)
            def _():
                remote(unit, unit, bfs.at[j], bfs.at[j], me.step(dc=1)).wait_send()

        for d in range(2):
            row_out(d).wait_send()
            row_on(d).wait_send()
        for h in range(2):
            fetch(h).wait_send()
            for d in range(2):
                across(h, d).wait_send()
                onto(h, d).wait_send()
            for k in range(4):
                share(h, k).wait_send()
        for copy in list(y_copies.values()) + shares + [last]:
            copy.wait_send()
        x_out.wait()
        w_out.wait()

    pl.run_scoped(sums, pltpu.VMEM((8, 2 * r, tokens), f32))


def fused(inputs, wt, cot):
    dma = pltpu.SemaphoreType.DMA
    vmem = pltpu.VMEM
    f32, bf16 = jnp.float32, jnp.bfloat16
    r, d = wt.shape
    t = inputs.shape[0]
    hbm = pl.BlockSpec(memory_space=pltpu.HBM)
    n, u = PIECES, UNITS
    return pl.pallas_call(
        kernel,
        out_shape=(
            jax.ShapeDtypeStruct((r, d), f32),
            jax.ShapeDtypeStruct((r, t), f32),
            jax.ShapeDtypeStruct((t, d), f32),
            jax.ShapeDtypeStruct((4, 2, r, d), f32),
            jax.ShapeDtypeStruct((4, r // n, d), f32),
        ),
        in_specs=[hbm] * 3,
        out_specs=(hbm,) * 5,
        scratch_shapes=[
            vmem((4 * r, 2 * d), bf16), vmem((4 * r, 2 * d), bf16), vmem((4 * r, t), bf16), vmem((4 * r, t), bf16),
            vmem((4, 2, r, d), f32), vmem((2, r, d), f32), vmem((2, 2, r, d), f32), vmem((2, r, d), f32),
            vmem((8, r, t), f32), vmem((2, 2, r, t // 2), f32), vmem((2, 2, r, t), f32), vmem((r, t), f32),
            dma((u,)), dma((2, u)), dma((u,)), dma((2, 2, u)), dma((2, 2, u)), dma((2, u)), dma((2, u)),
            dma((2,)), dma((2,)), dma((2, 2)), dma((2, 2)), dma((2, 2)), dma((2, 2)), dma((2, 4)), dma((2, 4)), dma((2,)),
            dma((2, n)), dma((2, n)), dma((2, 2, n)), dma((2, 2, n)), dma((n,)), dma((2, n)), dma((n,)),
            dma((8,)), dma((8,)), dma((2, 2)), dma((2, 2)), dma((2, 2, 2)), dma((2, 2, 2)), dma, dma,
            dma((2,)), dma((2,)), dma((2,)), dma((2,)), dma((4,)), dma((4, 2)), dma((4,)),
        ],
        compiler_params=pltpu.CompilerParams(collective_id=0, has_side_effects=True, vmem_limit_bytes=60 << 20),
    )(inputs, wt, cot)[:2]


def local(inputs, weight, cotangent):
    wout, xout = fused(inputs, weight.T, cotangent)
    return (xout.T, wout.T)


def solution(mesh):
    torus = Mesh(mesh.devices.reshape(4, 2, 2, 4, 2), AXES)
    in_specs = (P(("x", "zl"), "zh"), P("zh", ("y", "c", "x", "zl")), P(("x", "zl"), ("y", "c")))
    out_specs = (P(("x", "zl"), ("zh", "y", "c")), P("zh", ("y", "c", "x", "zl")))
    return jax.shard_map(local, mesh=torus, in_specs=in_specs, out_specs=out_specs, check_vma=False)
```
